32 devices in a mesh: slab: 4 (over y, core), inner: 8 (over z, x).
Axes of the slice: x: 2, y: 2, z: 4, core: 2. Of those that a mesh axis runs over, the one named last changes fastest.
Arguments:
- x_in: bfloat16 [8192, 16384], P(('slab', 'inner')), may hold values from -6 to 6
- bc_in: bfloat16 [8192, 4096], P(('slab', 'inner')), may hold values from -6 to 6
- dt_raw: bfloat16 [8192, 256], P(('slab', 'inner')), may hold values from -6.7 to -4.3
- dt_bias: float32 [256], replicated, may hold values from -0.5 to 0.5
- a_log: float32 [256], replicated, may hold values from -8 to 0, as said below
- d_skip: float32 [256], replicated, may hold values from 0.5 to 1.5
- conv_x_weight: float32 [4, 16384], replicated, may hold values from -3 to 3
- conv_x_bias: float32 [16384], replicated, may hold values from -3 to 3
- conv_bc_weight: float32 [4, 4096], replicated, may hold values from -3 to 3
- conv_bc_bias: float32 [4096], replicated, may hold values from -3 to 3
Outputs:
- y_out: bfloat16 [8192, 16384], P('slab', 'inner')
The draws below stay inside these ranges and needn't reach their ends.
Inputs may be any that keep to these rules, and one draw needn't show every extreme that they name: `a_log`: per-head logarithm of the decay rate.
All inputs are finite; a program needn't handle non-finite values.
Results may differ from the reference program's by a relative error of at most 0.0034.
Values may be sent and summed in bfloat16 or wider, within the bound.
No kernel may reach another device: no remote copies, remote signals or barrier semaphores. Data moves between devices by JAX's collectives and lax.ppermute only.
A program may use at most 256 MiB of HBM per device.

```python
import jax
import jax.numpy as jnp
from jax import lax

HEADS = 256
HEADDIM = 64
STATE = 256
GROUPS = 8
CONV = 4
SPAN = 256
INNER = 16384
SLAB_TOK = 2048
TOKENS = 8192
N_SLAB = 4


def draw_a_log(key, part):
    picked = jax.random.permutation(jax.random.fold_in(key, 11), HEADS)
    spread = jax.random.uniform(jax.random.fold_in(key, 12), (HEADS,), jnp.float32)
    fast_count = HEADS // 2
    fast_heads = picked < fast_count
    fast_rate = -1.6 + spread * 1.2
    slow_rate = jnp.log(0.2) + spread * jnp.log(5.0) - jnp.log(0.0041 * TOKENS)
    return jnp.where(fast_heads, fast_rate, slow_rate).astype(jnp.float32)


def draw_dt_raw(key, part):
    rough = jax.random.uniform(jax.random.fold_in(key, 21), (TOKENS, HEADS), jnp.float32, -0.8, 0.8)
    blocks = jax.random.uniform(jax.random.fold_in(key, 22), (TOKENS // SPAN, 1), jnp.float32, -0.35, 0.35)
    values = -5.5 + rough + jnp.repeat(blocks, SPAN, axis=0)
    return values.astype(jnp.bfloat16)


def block_scale(stream_key, extent, shards, least, top_value):
    factor_of, own = 1.0, jax.random.fold_in(stream_key, 6)
    for axis_at, shards_of in shards:
        draws = jnp.exp(jax.random.uniform(jax.random.fold_in(own, axis_at), (shards_of,), jnp.float32, least / len(shards), top_value / len(shards)))
        factor_of = factor_of * jnp.repeat(draws, extent[axis_at] // shards_of).reshape([-1 if axis == axis_at else 1 for axis in range(len(extent))])
    return factor_of


def gaussian(stream_key, extent, scale, limit, cuts=(), kind=jnp.bfloat16):
    array = scale * jax.random.normal(stream_key, extent, jnp.float32)
    if cuts:
        array = array * block_scale(stream_key, extent, cuts, -0.22, 0.18)
    return jnp.clip(array, -limit, limit).astype(kind)


def setup_inputs(seed: int = 0) -> dict:
    key_of = jax.random.split(jax.random.key(seed), 11)
    return {
        "x_in": gaussian(key_of[0], (TOKENS, INNER), 1.0, 6.0, ((0, 32),)),
        "bc_in": gaussian(key_of[1], (TOKENS, 2 * GROUPS * STATE), 1.0, 6.0, ((0, 32),)),
        "dt_raw": draw_dt_raw(jax.random.fold_in(key_of[10], 71), 0),
        "dt_bias": jnp.clip(jax.random.uniform(key_of[3], (HEADS,), jnp.float32, -0.5, 0.5), -0.5, 0.5),
        "a_log": draw_a_log(jax.random.fold_in(key_of[10], 71), 0),
        "d_skip": jnp.clip(jax.random.uniform(key_of[5], (HEADS,), jnp.float32, 0.5, 1.5), 0.5, 1.5),
        "conv_x_weight": gaussian(key_of[6], (CONV, INNER), CONV ** -0.5, 3.0, (), jnp.float32),
        "conv_x_bias": gaussian(key_of[7], (INNER,), 0.5, 3.0, (), jnp.float32),
        "conv_bc_weight": gaussian(key_of[8], (CONV, 2 * GROUPS * STATE), CONV ** -0.5, 3.0, (), jnp.float32),
        "conv_bc_bias": gaussian(key_of[9], (2 * GROUPS * STATE,), 0.5, 3.0, (), jnp.float32),
    }


def causal_conv(row_block, before, weight, conv_bias):
    kernel_len = weight.shape[0]
    length = row_block.shape[0]
    padded = jnp.concatenate([before, row_block], axis=0).astype(jnp.float32)
    summed = conv_bias[None, :] + weight[0][None, :] * padded[0:length]
    for offset in range(1, kernel_len):
        summed = summed + weight[offset][None, :] * padded[offset:offset + length]
    return jax.nn.silu(summed).astype(jnp.bfloat16)


def span_step(state, pieces):
    x_span, b_span, c_span, dt_span, da_span = pieces
    cumul = jnp.cumsum(da_span, axis=0).T
    size_q = cumul.shape[1]
    row_ids = lax.broadcasted_iota(jnp.int32, (size_q, size_q), 0)
    col_ids = lax.broadcasted_iota(jnp.int32, (size_q, size_q), 1)
    gaps = cumul[:, :, None] - cumul[:, None, :]
    decays = jnp.where((row_ids >= col_ids)[None], jnp.exp(jnp.minimum(gaps, 0.0)), 0.0)
    scores = jnp.dot(c_span, b_span.T, preferred_element_type=jnp.float32)
    mixing = (decays * scores[None] * dt_span.T[:, None, :]).astype(jnp.bfloat16)
    y_intra = jnp.einsum("hts,shp->thp", mixing.astype(jnp.float32), x_span.astype(jnp.float32))
    y_inter = jnp.einsum("tn,hnp->thp", c_span.astype(jnp.float32), state.astype(jnp.bfloat16).astype(jnp.float32))
    y_inter = y_inter * jnp.exp(cumul.T)[:, :, None]
    weights_end = (jnp.exp(cumul[:, -1:] - cumul) * dt_span.T).T
    scaled = (x_span.astype(jnp.float32) * weights_end[:, :, None]).astype(jnp.bfloat16)
    contrib = jnp.einsum("sn,shp->hnp", b_span.astype(jnp.float32), scaled.astype(jnp.float32))
    new_state = jnp.exp(cumul[:, -1])[:, None, None] * state + contrib
    return new_state, y_intra + y_inter


def slab_core(x_rows, b_rows, c_rows, dt_rows, da_rows):
    length = x_rows.shape[0]
    head_count = dt_rows.shape[1]
    span_count = length // SPAN
    inputs = (x_rows.reshape(span_count, SPAN, head_count, HEADDIM),
              b_rows.reshape(span_count, SPAN, STATE),
              c_rows.reshape(span_count, SPAN, STATE),
              dt_rows.reshape(span_count, SPAN, head_count),
              da_rows.reshape(span_count, SPAN, head_count))
    zero_state = jnp.zeros((head_count, STATE, HEADDIM), jnp.float32)
    end_state, outputs = lax.scan(span_step, zero_state, inputs)
    return outputs.reshape(length, head_count * HEADDIM), end_state


def reference(x_in, bc_in, dt_raw, dt_bias, a_log, d_skip, conv_x_weight, conv_x_bias, conv_bc_weight, conv_bc_bias):
    edge = CONV - 1
    bc_width = 2 * GROUPS * STATE
    x_slabs = x_in.reshape(N_SLAB, SLAB_TOK, INNER)
    bc_slabs = bc_in.reshape(N_SLAB, SLAB_TOK, bc_width)
    x_before = jnp.concatenate([jnp.zeros((1, edge, INNER), jnp.bfloat16), x_slabs[:-1, SLAB_TOK - edge:]], axis=0)
    bc_before = jnp.concatenate([jnp.zeros((1, edge, bc_width), jnp.bfloat16), bc_slabs[:-1, SLAB_TOK - edge:]], axis=0)
    dt_all = jax.nn.softplus(dt_raw.astype(jnp.float32) + dt_bias[None, :])
    da_all = dt_all * (-jnp.exp(a_log))[None, :]
    dt_slabs = dt_all.reshape(N_SLAB, SLAB_TOK, HEADS)
    da_slabs = da_all.reshape(N_SLAB, SLAB_TOK, HEADS)
    per_group = HEADS // GROUPS
    skip_cols = jnp.repeat(d_skip, HEADDIM)

    def one_slab(incoming, pieces):
        x_rows, x_prev, bc_rows, bc_prev, dt_rows, da_rows = pieces
        x_conv = causal_conv(x_rows, x_prev, conv_x_weight, conv_x_bias)
        bc_conv = causal_conv(bc_rows, bc_prev, conv_bc_weight, conv_bc_bias)
        y_parts = []
        end_parts = []
        for group_id in range(GROUPS):
            first = group_id * per_group
            y_part, end_part = slab_core(
                x_conv[:, first * HEADDIM:(first + per_group) * HEADDIM],
                bc_conv[:, group_id * STATE:(group_id + 1) * STATE],
                bc_conv[:, (GROUPS + group_id) * STATE:(GROUPS + group_id + 1) * STATE],
                dt_rows[:, first:first + per_group],
                da_rows[:, first:first + per_group])
            y_parts.append(y_part)
            end_parts.append(end_part)
        y_local = jnp.concatenate(y_parts, axis=1)
        end_local = jnp.concatenate(end_parts, axis=0)
        cum_slab = jnp.cumsum(da_rows, axis=0)
        c_groups = bc_conv[:, GROUPS * STATE:].reshape(SLAB_TOK, GROUPS, STATE).astype(jnp.float32)
        state_groups = incoming.astype(jnp.bfloat16).astype(jnp.float32).reshape(GROUPS, per_group, STATE, HEADDIM)
        carried = jnp.einsum("tgn,ghnp->tghp", c_groups, state_groups).reshape(SLAB_TOK, HEADS, HEADDIM)
        carried = carried * jnp.exp(cum_slab)[:, :, None]
        y_slab = y_local + carried.reshape(SLAB_TOK, INNER) + skip_cols[None, :] * x_conv.astype(jnp.float32)
        outgoing = jnp.exp(cum_slab[-1])[:, None, None] * incoming + end_local
        return outgoing, y_slab.astype(jnp.bfloat16)

    start_state = jnp.zeros((HEADS, STATE, HEADDIM), jnp.float32)
    last_state, y_all = lax.scan(one_slab, start_state, (x_slabs, x_before, bc_slabs, bc_before, dt_slabs, da_slabs))
    return y_all.reshape(TOKENS, INNER)
```

```python
import functools

import jax
import jax.numpy as jnp
from jax import lax
from jax.experimental import pallas as pl
from jax.experimental.pallas import tpu as pltpu
from jax.sharding import PartitionSpec as P

HEADS = 256
HEADDIM = 64
STATE = 256
GROUPS = 8
CONV = 4
LANES = 128
EDGE_ROWS = 8
SEG = 16


F32 = jnp.float32
BF16 = jnp.bfloat16
ANY = pl.BlockSpec(memory_space=pl.ANY)


def whole(shape):
    return pl.BlockSpec(shape, lambda *_: (0,) * len(shape))


def params(mib=48):
    return pltpu.CompilerParams(vmem_limit_bytes=mib << 20)


def cost(flops, moved):
    return pl.CostEstimate(flops=flops, bytes_accessed=moved, transcendentals=0)


def chunk_widths(channels):
    widths, left = [], channels
    while left > LANES:
        widths.append(max(left // 2, LANES))
        left -= widths[-1]
    return widths + [left]


def silu(x):
    half = 0.5 * x
    return half + half * jnp.tanh(half)


def conv_rows(carry, rows, weight, bias):
    ext = jnp.concatenate([carry, rows], axis=0)
    acc = bias + weight[CONV - 1 : CONV] * rows
    for back in range(1, CONV):
        shifted = pltpu.roll(ext, back, 0)[EDGE_ROWS:]
        acc = acc + weight[CONV - 1 - back : CONV - back] * shifted
    return silu(acc).astype(BF16)


def spread(per_head, heads_dev, first, width):
    return jnp.dot(per_head, pick(heads_dev, first, width), preferred_element_type=F32)


def pick(heads_dev, first, width):
    row = lax.broadcasted_iota(jnp.int32, (LANES, width), 0)
    col = lax.broadcasted_iota(jnp.int32, (LANES, width), 1)
    head = first + col // HEADDIM
    hit = (row == head) | (row == head + heads_dev)
    return jnp.where(hit, 1.0, 0.0).astype(BF16)


def pack_bc(me, bc_in, dt_raw, n, heads_dev, per_group):
    tok = bc_in.shape[0]

    def body(me_ref, *refs):
        b_refs, c_refs, dt_ref = refs[:n], refs[n : 2 * n], refs[2 * n]
        outs, turned = refs[2 * n + 1 : 3 * n + 1], refs[3 * n + 1]
        turned[...] = dt_ref[...].astype(F32).T
        for s in range(n):
            outs[s][:tok, :STATE] = b_refs[s][...]
            outs[s][:tok, STATE:] = c_refs[s][...]
            first = pl.multiple_of(((me_ref[0] + s) % n) * heads_dev, heads_dev)
            dt_s = turned[pl.ds(first, heads_dev), :].astype(BF16)
            for seg in range(2):
                if seg * SEG < heads_dev:
                    part = dt_s[seg * SEG : (seg + 1) * SEG]
                else:
                    part = jnp.zeros((SEG, tok), BF16)
                outs[s][tok:, seg * tok : (seg + 1) * tok] = part

    def column(s, base):
        return lambda i, me: (0, base + ((me[0] + s) % n) * heads_dev // per_group)

    rows = tok + SEG
    return pl.pallas_call(
        body,
        grid_spec=pltpu.PrefetchScalarGridSpec(
            num_scalar_prefetch=1,
            grid=(1,),
            in_specs=[pl.BlockSpec((tok, STATE), column(s, 0)) for s in range(n)]
            + [pl.BlockSpec((tok, STATE), column(s, GROUPS)) for s in range(n)]
            + [whole(dt_raw.shape)],
            out_specs=[whole((rows, 2 * STATE))] * n,
            scratch_shapes=[pltpu.VMEM(dt_raw.shape[::-1], F32)],
        ),
        out_shape=[jax.ShapeDtypeStruct((rows, 2 * STATE), BF16)] * n,
        compiler_params=params(),
        cost_estimate=cost(0, 4 * bc_in.size),
        name="pack_bc",
    )(me, *([bc_in] * (2 * n)), dt_raw)


def pack_x(me, x_in, n, channels, width, first):
    tok = x_in.shape[0]
    step = min(64, tok)
    per = channels // width

    def body(me_ref, *refs):
        for s in range(n - 1):
            refs[n - 1 + s][...] = refs[s][...]

    def column(s):
        return lambda i, me: (i, ((me[0] + s) % n) * per + first // width)

    return pl.pallas_call(
        body,
        grid_spec=pltpu.PrefetchScalarGridSpec(
            num_scalar_prefetch=1,
            grid=(tok // step,),
            in_specs=[pl.BlockSpec((step, width), column(s)) for s in range(1, n)],
            out_specs=[pl.BlockSpec((step, width), lambda i, me: (i, 0))] * (n - 1),
        ),
        out_shape=[jax.ShapeDtypeStruct((tok, width), BF16)] * (n - 1),
        compiler_params=params(),
        cost_estimate=cost(0, 4 * tok * width * (n - 1)),
        name="pack_x",
    )(me, *([x_in] * (n - 1)))


def pack_edge(x_in, bc_in, n, channels, heads_dev, per_group):
    tok = x_in.shape[0]
    wide = channels + 2 * STATE

    def body(x_ref, bc_ref, *outs):
        x = x_ref[...].astype(F32)[EDGE_ROWS:].astype(BF16)
        bc = bc_ref[...].astype(F32)[EDGE_ROWS:].astype(BF16)
        for j in range(n):
            g = j * heads_dev // per_group
            outs[j][:, :channels] = x[:, j * channels : (j + 1) * channels]
            outs[j][:, channels : channels + STATE] = bc[:, g * STATE : (g + 1) * STATE]
            g += GROUPS
            outs[j][:, channels + STATE :] = bc[:, g * STATE : (g + 1) * STATE]

    last = tok // (2 * EDGE_ROWS) - 1
    return pl.pallas_call(
        body,
        grid=(1,),
        in_specs=[
            pl.BlockSpec((2 * EDGE_ROWS, x_in.shape[1]), lambda i: (last, 0)),
            pl.BlockSpec((2 * EDGE_ROWS, bc_in.shape[1]), lambda i: (last, 0)),
        ],
        out_specs=[whole((EDGE_ROWS, wide))] * n,
        out_shape=[jax.ShapeDtypeStruct((EDGE_ROWS, wide), BF16)] * n,
        compiler_params=params(),
        cost_estimate=cost(0, 4 * EDGE_ROWS * wide * n),
        name="pack_edge",
    )(x_in, bc_in)


def prepare(me, messages, edge, weight, bias, dt_bias, a_log, n, heads_dev, per_group):
    rows = messages[0].shape[0]
    tok = rows - SEG
    total = n * tok

    def body(me_ref, *refs):
        msgs, refs = refs[:n], refs[n:]
        edge_ref, wb_ref, wc_ref, bb_ref, bc_ref, dtb_ref, al_ref = refs[:7]
        bt_out, c_out, m_out, wu_out, wv_out, ec_out, dv_out = refs[7:14]
        buf, cum_s, dt_s, sems = refs[14:]
        copies = []
        for s in range(n):
            j = lax.rem(me_ref[0] - s + n, n)
            copies.append(pltpu.make_async_copy(msgs[s], buf.at[j], sems.at[s]))
            copies[-1].start()
        for copy in copies:
            copy.wait()

        def split(w):
            hi = w.astype(BF16).astype(F32)
            parts = [hi, w - hi]
            if 2 * heads_dev < LANES:
                parts.append(jnp.zeros((LANES - 2 * heads_dev, w.shape[1]), F32))
            return jnp.concatenate(parts, axis=0)

        at = lax.broadcasted_iota(jnp.int32, (tok, tok), 0)
        to = lax.broadcasted_iota(jnp.int32, (tok, tok), 1)
        upto = jnp.where(at <= to, 1.0, 0.0).astype(F32)
        rate = -jnp.exp(al_ref[...])
        ends = []
        for j in range(n):
            dt_raw = buf[j, tok:, :].astype(F32)
            segs = [dt_raw[:, i * tok : (i + 1) * tok] for i in range(heads_dev // SEG)]
            dt = jax.nn.softplus(jnp.concatenate(segs, axis=0) + dtb_ref[...])
            cum = jnp.dot(
                dt * rate,
                upto,
                precision=lax.Precision.HIGHEST,
                preferred_element_type=F32,
            )
            dt_s[j] = dt
            cum_s[j] = cum
            ends.append(cum[:, tok - 1 :])
        after = jnp.zeros_like(ends[0])
        for j in reversed(range(n)):
            dt, cum = dt_s[j], cum_s[j]
            here = pl.ds(j * tok, tok)
            wu_out[here, :] = split(dt * jnp.exp(-cum)).T.astype(BF16)
            wv_out[here, :] = split(dt * jnp.exp(after + ends[j] - cum)).T.astype(BF16)
            ec_out[here, :] = split(jnp.exp(cum)).T.astype(BF16)
            after = after + ends[j]
        decay = jnp.broadcast_to(jnp.exp(after), (heads_dev, LANES))
        dv_out[...] = split(decay).T.astype(BF16)[: dv_out.shape[0]]

        strip = 32
        lower = at >= to

        def block(j, carry):
            def step(i, carry):
                r = pl.multiple_of(i * strip, strip)
                x = buf[j, pl.ds(r, strip), :].astype(F32)
                new = []
                for half, w_ref, b_ref in ((0, wb_ref, bb_ref), (1, wc_ref, bc_ref)):
                    mine = x[:, half * STATE : (half + 1) * STATE]
                    done = conv_rows(carry[half], mine, w_ref[...], b_ref[...])
                    buf[j, pl.ds(r, strip), half * STATE : (half + 1) * STATE] = done
                    new.append(mine[strip - EDGE_ROWS :])
                return tuple(new)

            carry = lax.fori_loop(0, tok // strip, step, carry)
            b, c = buf[j, :tok, :STATE], buf[j, :tok, STATE:]
            t = pl.multiple_of(j * tok, tok)
            turned = b.astype(F32).T.astype(BF16)
            bt_out[:, pl.ds(t, tok)] = turned
            c_out[pl.ds(t, tok), :] = c
            scores = jnp.dot(c, turned, preferred_element_type=F32)
            m_out[pl.ds(t, tok), :] = jnp.where(lower, scores, 0.0).astype(BF16)
            return carry

        e = edge_ref[...].astype(F32)
        lax.fori_loop(0, n, block, (e[:, :STATE], e[:, STATE:]))

    def group(base):
        return lambda i, me: (0, base + me[0] * heads_dev // per_group)

    vec = (heads_dev, 1)
    shapes = [
        (STATE, total),
        (total, STATE),
        (total, tok),
        (total, LANES),
        (total, LANES),
        (total, LANES),
        (2 * EDGE_ROWS, LANES),
    ]
    return pl.pallas_call(
        body,
        grid_spec=pltpu.PrefetchScalarGridSpec(
            num_scalar_prefetch=1,
            grid=(1,),
            in_specs=[ANY] * n
            + [
                whole(edge.shape),
                pl.BlockSpec((CONV, STATE), group(0)),
                pl.BlockSpec((CONV, STATE), group(GROUPS)),
                pl.BlockSpec((1, STATE), group(0)),
                pl.BlockSpec((1, STATE), group(GROUPS)),
                whole(vec),
                whole(vec),
            ],
            out_specs=[whole(s) for s in shapes],
            scratch_shapes=[
                pltpu.VMEM((n, rows, 2 * STATE), BF16),
                pltpu.VMEM((n, heads_dev, tok), F32),
                pltpu.VMEM((n, heads_dev, tok), F32),
                pltpu.SemaphoreType.DMA((n,)),
            ],
        ),
        out_shape=[jax.ShapeDtypeStruct(s, BF16) for s in shapes],
        compiler_params=params(),
        cost_estimate=cost(4 * total * STATE * tok, 20 * total * STATE),
        name="prepare",
    )(me, *messages, edge, weight, weight, bias, bias, dt_bias, a_log)


def convolve(me, x_in, received, edge, weight, bias, bt, wv, n, heads_dev, channels, width, first):
    tok = x_in.shape[0]
    total = n * tok
    per = channels // width
    group = min(width, 256)
    strip = 32

    def body(me_ref, x_ref, *refs):
        got, refs = refs[: n - 1], refs[n - 1 :]
        edge_ref, w_ref, b_ref, bt_ref, wv_ref, xc_ref, end_ref, buf, scale, sems, out_sems = refs
        copies = []
        for s in range(n):
            j = lax.rem(me_ref[0] - s + n, n)
            if s:
                src = got[s - 1]
            else:
                col = pl.multiple_of(me_ref[0] * channels + first, LANES)
                src = x_ref.at[:, pl.ds(col, width)]
            copies.append(pltpu.make_async_copy(src, buf.at[j], sems.at[s]))
            copies[-1].start()
        for copy in copies:
            copy.wait()
        end_ref[...] = jnp.zeros_like(end_ref)

        def block(j, carry):
            t = pl.multiple_of(j * tok, tok)
            scale[...] = spread(wv_ref[pl.ds(t, tok), :], heads_dev, first // HEADDIM, width)

            def step(i, carry):
                r = pl.multiple_of(i * strip, strip)
                new = []
                for g in range(width // group):
                    cols = slice(g * group, (g + 1) * group)
                    x = buf[j, pl.ds(r, strip), cols].astype(F32)
                    xc = conv_rows(carry[g], x, w_ref[:, cols], b_ref[:, cols])
                    buf[j, pl.ds(r, strip), cols] = xc
                    v = xc.astype(F32) * scale[pl.ds(r, strip), cols]
                    scale[pl.ds(r, strip), cols] = v
                    new.append(x[strip - EDGE_ROWS :])
                return tuple(new)

            carry = lax.fori_loop(0, tok // strip, step, carry)
            pltpu.make_async_copy(buf.at[j], xc_ref.at[pl.ds(t, tok), :], out_sems.at[j]).start()
            lhs = bt_ref[:, pl.ds(t, tok)]
            for g in range(width // group):
                cols = slice(g * group, (g + 1) * group)
                v = scale[:, cols].astype(BF16)
                end_ref[:, cols] += jnp.dot(lhs, v, preferred_element_type=F32)
            return carry

        e = edge_ref[...].astype(F32)
        lax.fori_loop(
            0, n, block, tuple(e[:, g * group : (g + 1) * group] for g in range(width // group))
        )
        for j in range(n):
            pltpu.make_async_copy(
                buf.at[j], xc_ref.at[pl.ds(j * tok, tok), :], out_sems.at[j]
            ).wait()

    return pl.pallas_call(
        body,
        grid_spec=pltpu.PrefetchScalarGridSpec(
            num_scalar_prefetch=1,
            grid=(1,),
            in_specs=[ANY] * n
            + [
                pl.BlockSpec((EDGE_ROWS, width), lambda i, me: (0, first // width)),
                pl.BlockSpec((CONV, width), lambda i, me: (0, me[0] * per + first // width)),
                pl.BlockSpec((1, width), lambda i, me: (0, me[0] * per + first // width)),
                whole(bt.shape),
                whole(wv.shape),
            ],
            out_specs=[ANY, whole((STATE, width))],
            scratch_shapes=[
                pltpu.VMEM((n, tok, width), BF16),
                pltpu.VMEM((tok, width), F32),
                pltpu.SemaphoreType.DMA((n,)),
                pltpu.SemaphoreType.DMA((n,)),
            ],
        ),
        out_shape=[
            jax.ShapeDtypeStruct((total, width), BF16),
            jax.ShapeDtypeStruct((STATE, width), F32),
        ],
        compiler_params=params(),
        cost_estimate=cost(2 * total * STATE * width, 4 * total * width + 4 * total * STATE),
        name="convolve",
    )(me, x_in, *received, edge, weight, bias, bt, wv)


def emit(y, xc, bt, c, m, wu, ec, ends, decays, skip, heads_dev, channels, width, first):
    total = xc.shape[0]
    tok = m.shape[1]
    group = min(width, 256)
    n_ends, n_decays = len(ends), len(decays)
    alias = [] if y is None else [y]

    def body(*refs):
        refs = refs[len(alias) :]
        xc_ref, bt_ref, c_ref, m_ref, wu_ref, ec_ref, skip_ref = refs[:7]
        end_refs, refs = refs[7 : 7 + n_ends], refs[7 + n_ends :]
        decay_refs, (out_ref, state) = refs[:n_decays], refs[n_decays:]

        @pl.when(pl.program_id(0) == 0)
        def _():
            carried = end_refs[-1][...].astype(F32)
            for i in reversed(range(n_ends - 1)):
                d = spread(decay_refs[i][...], heads_dev, first // HEADDIM, width)[:1]
                carried = end_refs[i][...].astype(F32) + d * carried
            state[...] = carried

        for g in range(width // group):
            cols = slice(g * group, (g + 1) * group)
            head = first // HEADDIM + g * (group // HEADDIM)
            x = xc_ref[:, cols].astype(F32)
            u = (x * spread(wu_ref[...], heads_dev, head, group)).astype(BF16)
            e = spread(ec_ref[...], heads_dev, head, group)
            s = state[:, cols]
            y_g = jnp.dot(m_ref[...], u, preferred_element_type=F32)
            y_g += jnp.dot(c_ref[...], s.astype(BF16), preferred_element_type=F32)
            out_ref[:, cols] = (e * y_g + skip_ref[:, cols] * x).astype(BF16)
            s = s + jnp.dot(bt_ref[...], u, preferred_element_type=F32)
            state[:, cols] = e[tok - 1 :] * s

    row = lambda j: (j, 0)
    return pl.pallas_call(
        body,
        grid=(total // tok,),
        in_specs=[ANY] * len(alias)
        + [
            pl.BlockSpec((tok, width), row),
            pl.BlockSpec((STATE, tok), lambda j: (0, j)),
            pl.BlockSpec((tok, STATE), row),
            pl.BlockSpec((tok, tok), row),
            pl.BlockSpec((tok, LANES), row),
            pl.BlockSpec((tok, LANES), row),
            pl.BlockSpec((1, width), lambda j: (0, first // width)),
        ]
        + [whole((STATE, width))] * n_ends
        + [whole((2 * EDGE_ROWS, LANES))] * n_decays,
        out_specs=pl.BlockSpec((tok, width), lambda j: (j, first // width)),
        out_shape=jax.ShapeDtypeStruct((total, channels), BF16),
        scratch_shapes=[pltpu.VMEM((STATE, width), F32)],
        input_output_aliases={0: 0} if alias else {},
        compiler_params=params(),
        cost_estimate=cost(6 * total * STATE * width, 4 * total * width + 6 * total * STATE),
        name="emit",
    )(*alias, xc, bt, c, m, wu, ec, skip, *ends, *decays)


def shards(
    x_in,
    bc_in,
    dt_raw,
    dt_bias,
    a_log,
    d_skip,
    conv_x_weight,
    conv_x_bias,
    conv_bc_weight,
    conv_bc_bias,
):
    n = lax.axis_size("inner")
    n_slab = lax.axis_size("slab")
    heads_dev = HEADS // n
    channels = heads_dev * HEADDIM
    per_group = HEADS // GROUPS
    index = lax.axis_index("inner")
    me = index.astype(jnp.int32).reshape(1)

    def rotate(arrays, first_shift=1):
        return [
            lax.ppermute(a, "inner", [(i, (i + s) % n) for i in range(n)])
            for s, a in enumerate(arrays, first_shift)
        ]

    def forward(a, by):
        return lax.ppermute(a, "slab", [(i, i + by) for i in range(n_slab - by)])

    packed = pack_bc(me, bc_in, dt_raw, n, heads_dev, per_group)
    messages = [packed[0]] + rotate(packed[1:])
    widths = chunk_widths(channels)
    chunks, first = [], 0
    for width in widths:
        chunks.append((width, first, rotate(pack_x(me, x_in, n, channels, width, first))))
        first += width
    edges = pack_edge(x_in, bc_in, n, channels, heads_dev, per_group)
    edge = sum(
        lax.ppermute(
            e, ("slab", "inner"), [(s * n + n - 1, (s + 1) * n + j) for s in range(n_slab - 1)]
        )
        for j, e in enumerate(edges)
    )

    def mine(v):
        return lax.dynamic_slice_in_dim(v, index * heads_dev, heads_dev, 0)

    skip = jnp.repeat(mine(d_skip), HEADDIM)[None, :]
    bt, c, m, wu, wv, ec, dv = prepare(
        me,
        messages,
        edge[:, channels:],
        conv_bc_weight,
        conv_bc_bias[None, :],
        mine(dt_bias)[:, None],
        mine(a_log)[:, None],
        n,
        heads_dev,
        per_group,
    )
    decays = [forward(dv, by) for by in range(1, n_slab - 1)]
    y = None
    for width, first, received in chunks:
        xc, end = convolve(
            me,
            x_in,
            received,
            edge,
            conv_x_weight,
            conv_x_bias[None, :],
            bt,
            wv,
            n,
            heads_dev,
            channels,
            width,
            first,
        )
        end = end.astype(BF16)
        ends = [forward(end, by) for by in range(1, n_slab)]
        y = emit(y, xc, bt, c, m, wu, ec, ends, decays, skip, heads_dev, channels, width, first)
    return y


def solution(mesh):
    tokens = P(("slab", "inner"), None)
    placed = (tokens, tokens, tokens) + (P(),) * 7
    return jax.shard_map(
        shards, mesh=mesh, in_specs=placed, out_specs=P("slab", "inner"), check_vma=False
    )
```

```python
import jax
import jax.numpy as jnp
from jax import lax
from jax.experimental import pallas as pl
from jax.experimental.pallas import tpu as pltpu
from jax.sharding import PartitionSpec as P


HEADS = 256
HEADDIM = 64
STATE = 256
GROUPS = 8
CONV = 4
LANES = 128
EDGE_ROWS = 8
SENT_ROWS = 4
SEG = 16


F32 = jnp.float32
BF16 = jnp.bfloat16
ANY = pl.BlockSpec(memory_space=pl.ANY)


def whole(shape):
    return pl.BlockSpec(shape, lambda *_: (0,) * len(shape))


def params():
    return pltpu.CompilerParams(vmem_limit_bytes=63 << 20)


def cost(flops, moved):
    return pl.CostEstimate(flops=flops, bytes_accessed=moved, transcendentals=0)


def chunk_widths(channels):
    return [channels // 4] * 4


def rows_ahead(edge_ref):
    e = edge_ref[...].astype(F32)
    return jnp.concatenate([jnp.zeros((EDGE_ROWS - SENT_ROWS, e.shape[1]), F32), e], axis=0)


def silu(x):
    half = 0.5 * x
    return half + half * jnp.tanh(half)


def conv_rows(carry, rows, weight, bias):
    ext = jnp.concatenate([carry, rows], axis=0)
    acc = bias + weight[CONV - 1 : CONV] * rows
    for back in range(1, CONV):
        shifted = pltpu.roll(ext, back, 0)[EDGE_ROWS:]
        acc = acc + weight[CONV - 1 - back : CONV - back] * shifted
    return silu(acc).astype(BF16)


def spread(per_head, heads_dev, first, width):
    return jnp.dot(per_head, pick(heads_dev, first, width), preferred_element_type=F32)


def pick(heads_dev, first, width):
    row = lax.broadcasted_iota(jnp.int32, (LANES, width), 0)
    col = lax.broadcasted_iota(jnp.int32, (LANES, width), 1)
    head = first + col // HEADDIM
    hit = (row == head) | (row == head + heads_dev)
    return jnp.where(hit, 1.0, 0.0).astype(BF16)


def pack_bc(me, bc_in, dt_raw, n, heads_dev, per_group):
    tok = bc_in.shape[0]

    def body(me_ref, *refs):
        b_refs, c_refs, dt_ref = refs[:n], refs[n : 2 * n], refs[2 * n]
        outs, turned = refs[2 * n + 1 : 3 * n + 1], refs[3 * n + 1]
        turned[...] = dt_ref[...].astype(F32).T
        for s in range(n):
            outs[s][:tok, :STATE] = b_refs[s][...]
            outs[s][:tok, STATE:] = c_refs[s][...]
            first = pl.multiple_of(((me_ref[0] + s) % n) * heads_dev, heads_dev)
            dt_s = turned[pl.ds(first, heads_dev), :].astype(BF16)
            for seg in range(2):
                if seg * SEG < heads_dev:
                    part = dt_s[seg * SEG : (seg + 1) * SEG]
                else:
                    part = jnp.zeros((SEG, tok), BF16)
                outs[s][tok:, seg * tok : (seg + 1) * tok] = part

    def column(s, base):
        return lambda i, me: (0, base + ((me[0] + s) % n) * heads_dev // per_group)

    rows = tok + SEG
    return pl.pallas_call(
        body,
        grid_spec=pltpu.PrefetchScalarGridSpec(
            num_scalar_prefetch=1,
            grid=(1,),
            in_specs=[pl.BlockSpec((tok, STATE), column(s, 0)) for s in range(n)]
            + [pl.BlockSpec((tok, STATE), column(s, GROUPS)) for s in range(n)]
            + [whole(dt_raw.shape)],
            out_specs=[whole((rows, 2 * STATE))] * n,
            scratch_shapes=[pltpu.VMEM(dt_raw.shape[::-1], F32)],
        ),
        out_shape=[jax.ShapeDtypeStruct((rows, 2 * STATE), BF16)] * n,
        compiler_params=params(),
        cost_estimate=cost(0, 4 * bc_in.size),
        name="pack_bc",
    )(me, *([bc_in] * (2 * n)), dt_raw)


def pack_x(me, x_in, n, channels, width, first, after):
    tok = x_in.shape[0]
    step = min(64, tok)
    per = channels // width

    def body(me_ref, *refs):
        outs = refs[n - 1 + len(after) :]
        for s in range(n - 1):
            outs[s][...] = refs[s][...]

    def column(s):
        return lambda i, me: (i, ((me[0] + s) % n) * per + first // width)

    return pl.pallas_call(
        body,
        grid_spec=pltpu.PrefetchScalarGridSpec(
            num_scalar_prefetch=1,
            grid=(tok // step,),
            in_specs=[pl.BlockSpec((step, width), column(s)) for s in range(1, n)]
            + [ANY] * len(after),
            out_specs=[pl.BlockSpec((step, width), lambda i, me: (i, 0))] * (n - 1),
        ),
        out_shape=[jax.ShapeDtypeStruct((tok, width), BF16)] * (n - 1),
        compiler_params=params(),
        cost_estimate=cost(0, 4 * tok * width * (n - 1)),
        name="pack_x",
    )(me, *([x_in] * (n - 1)), *after)


def pack_edge(x_in, bc_in, n, channels, heads_dev, per_group):
    tok = x_in.shape[0]
    wide = channels + 2 * STATE

    def body(x_ref, bc_ref, *outs):
        x = x_ref[...].astype(F32)[2 * EDGE_ROWS - SENT_ROWS :].astype(BF16)
        bc = bc_ref[...].astype(F32)[2 * EDGE_ROWS - SENT_ROWS :].astype(BF16)
        for j in range(n):
            g = j * heads_dev // per_group
            outs[j][:, :channels] = x[:, j * channels : (j + 1) * channels]
            outs[j][:, channels : channels + STATE] = bc[:, g * STATE : (g + 1) * STATE]
            g += GROUPS
            outs[j][:, channels + STATE :] = bc[:, g * STATE : (g + 1) * STATE]

    last = tok // (2 * EDGE_ROWS) - 1
    return pl.pallas_call(
        body,
        grid=(1,),
        in_specs=[
            pl.BlockSpec((2 * EDGE_ROWS, x_in.shape[1]), lambda i: (last, 0)),
            pl.BlockSpec((2 * EDGE_ROWS, bc_in.shape[1]), lambda i: (last, 0)),
        ],
        out_specs=[whole((SENT_ROWS, wide))] * n,
        out_shape=[jax.ShapeDtypeStruct((SENT_ROWS, wide), BF16)] * n,
        compiler_params=params(),
        cost_estimate=cost(0, 4 * EDGE_ROWS * wide * n),
        name="pack_edge",
    )(x_in, bc_in)


def prepare(me, messages, edge, weight, bias, dt_bias, a_log, n, heads_dev, per_group):
    rows = messages[0].shape[0]
    tok = rows - SEG
    total = n * tok

    def body(me_ref, *refs):
        msgs, refs = refs[:n], refs[n:]
        edge_ref, wb_ref, wc_ref, bb_ref, bc_ref, dtb_ref, al_ref = refs[:7]
        bt_out, c_out, m_out, wu_out, wv_out, ec_out, dv_out = refs[7:14]
        buf, cum_s, dt_s, sems = refs[14:]
        copies = []
        for s in range(n):
            j = lax.rem(me_ref[0] - s + n, n)
            copies.append(pltpu.make_async_copy(msgs[s], buf.at[j], sems.at[s]))
            copies[-1].start()
        for copy in copies:
            copy.wait()

        def split(w):
            hi = w.astype(BF16).astype(F32)
            parts = [hi, w - hi]
            if 2 * heads_dev < LANES:
                parts.append(jnp.zeros((LANES - 2 * heads_dev, w.shape[1]), F32))
            return jnp.concatenate(parts, axis=0)

        at = lax.broadcasted_iota(jnp.int32, (tok, tok), 0)
        to = lax.broadcasted_iota(jnp.int32, (tok, tok), 1)
        upto = jnp.where(at <= to, 1.0, 0.0).astype(F32)
        rate = -jnp.exp(al_ref[...])
        ends = []
        for j in range(n):
            dt_raw = buf[j, tok:, :].astype(F32)
            segs = [dt_raw[:, i * tok : (i + 1) * tok] for i in range(heads_dev // SEG)]
            dt = jax.nn.softplus(jnp.concatenate(segs, axis=0) + dtb_ref[...])
            cum = jnp.dot(
                dt * rate,
                upto,
                precision=lax.Precision.HIGHEST,
                preferred_element_type=F32,
            )
            dt_s[j] = dt
            cum_s[j] = cum
            ends.append(cum[:, tok - 1 :])
        after = jnp.zeros_like(ends[0])
        for j in reversed(range(n)):
            dt, cum = dt_s[j], cum_s[j]
            here = pl.ds(j * tok, tok)
            wu_out[here, :] = split(dt * jnp.exp(-cum)).T.astype(BF16)
            wv_out[here, :] = split(dt * jnp.exp(after + ends[j] - cum)).T.astype(BF16)
            ec_out[here, :] = split(jnp.exp(cum)).T.astype(BF16)
            after = after + ends[j]
        decay = jnp.broadcast_to(jnp.exp(after), (heads_dev, LANES))
        dv_out[...] = split(decay).T.astype(BF16)[: dv_out.shape[0]]

        strip = 32
        lower = at >= to

        def block(j, carry):
            def step(i, carry):
                r = pl.multiple_of(i * strip, strip)
                x = buf[j, pl.ds(r, strip), :].astype(F32)
                new = []
                for half, w_ref, b_ref in ((0, wb_ref, bb_ref), (1, wc_ref, bc_ref)):
                    mine = x[:, half * STATE : (half + 1) * STATE]
                    done = conv_rows(carry[half], mine, w_ref[...], b_ref[...])
                    buf[j, pl.ds(r, strip), half * STATE : (half + 1) * STATE] = done
                    new.append(mine[strip - EDGE_ROWS :])
                return tuple(new)

            carry = lax.fori_loop(0, tok // strip, step, carry)
            b, c = buf[j, :tok, :STATE], buf[j, :tok, STATE:]
            t = pl.multiple_of(j * tok, tok)
            turned = b.astype(F32).T.astype(BF16)
            bt_out[:, pl.ds(t, tok)] = turned
            c_out[pl.ds(t, tok), :] = c
            scores = jnp.dot(c, turned, preferred_element_type=F32)
            m_out[pl.ds(t, tok), :] = jnp.where(lower, scores, 0.0).astype(BF16)
            return carry

        e = rows_ahead(edge_ref)
        lax.fori_loop(0, n, block, (e[:, :STATE], e[:, STATE:]))

    def group(base):
        return lambda i, me: (0, base + me[0] * heads_dev // per_group)

    vec = (heads_dev, 1)
    shapes = [
        (STATE, total),
        (total, STATE),
        (total, tok),
        (total, LANES),
        (total, LANES),
        (total, LANES),
        (2 * EDGE_ROWS, LANES),
    ]
    return pl.pallas_call(
        body,
        grid_spec=pltpu.PrefetchScalarGridSpec(
            num_scalar_prefetch=1,
            grid=(1,),
            in_specs=[ANY] * n
            + [
                whole(edge.shape),
                pl.BlockSpec((CONV, STATE), group(0)),
                pl.BlockSpec((CONV, STATE), group(GROUPS)),
                pl.BlockSpec((1, STATE), group(0)),
                pl.BlockSpec((1, STATE), group(GROUPS)),
                whole(vec),
                whole(vec),
            ],
            out_specs=[whole(s) for s in shapes],
            scratch_shapes=[
                pltpu.VMEM((n, rows, 2 * STATE), BF16),
                pltpu.VMEM((n, heads_dev, tok), F32),
                pltpu.VMEM((n, heads_dev, tok), F32),
                pltpu.SemaphoreType.DMA((n,)),
            ],
        ),
        out_shape=[jax.ShapeDtypeStruct(s, BF16) for s in shapes],
        compiler_params=params(),
        cost_estimate=cost(4 * total * STATE * tok, 20 * total * STATE),
        name="prepare",
    )(me, *messages, edge, weight, weight, bias, bias, dt_bias, a_log)


def convolve(me, x_in, received, edge, weight, bias, bt, wv, n, heads_dev, channels, width, first, after):
    tok = x_in.shape[0]
    total = n * tok
    per = channels // width
    group = min(width, 256)
    strip = min(tok, 64 * 256 // group)

    def body(me_ref, x_ref, *refs):
        got, refs = refs[: n - 1], refs[n - 1 :]
        edge_ref, w_ref, b_ref, bt_ref, wv_ref = refs[:5]
        xc_ref, end_out, buf, scale, end_ref, sems, out_sems = refs[5 + len(after) :]
        copies = []
        for s in range(n):
            j = lax.rem(me_ref[0] - s + n, n)
            if s:
                src = got[s - 1]
            else:
                col = pl.multiple_of(me_ref[0] * channels + first, LANES)
                src = x_ref.at[:, pl.ds(col, width)]
            copies.append(pltpu.make_async_copy(src, buf.at[j], sems.at[s]))
            copies[-1].start()
        for copy in copies:
            copy.wait()
        end_ref[...] = jnp.zeros_like(end_ref)

        def block(j, carry):
            t = pl.multiple_of(j * tok, tok)
            scale[...] = spread(wv_ref[pl.ds(t, tok), :], heads_dev, first // HEADDIM, width)

            def step(i, carry):
                r = pl.multiple_of(i * strip, strip)
                new = []
                for g in range(width // group):
                    cols = slice(g * group, (g + 1) * group)
                    x = buf[j, pl.ds(r, strip), cols].astype(F32)
                    xc = conv_rows(carry[g], x, w_ref[:, cols], b_ref[:, cols])
                    buf[j, pl.ds(r, strip), cols] = xc
                    v = xc.astype(F32) * scale[pl.ds(r, strip), cols]
                    scale[pl.ds(r, strip), cols] = v
                    new.append(x[strip - EDGE_ROWS :])
                return tuple(new)

            carry = lax.fori_loop(0, tok // strip, step, carry)
            pltpu.make_async_copy(buf.at[j], xc_ref.at[pl.ds(t, tok), :], out_sems.at[j]).start()
            lhs = bt_ref[:, pl.ds(t, tok)]
            for g in range(width // group):
                cols = slice(g * group, (g + 1) * group)
                v = scale[:, cols].astype(BF16)
                end_ref[:, cols] += jnp.dot(lhs, v, preferred_element_type=F32)
            return carry

        e = rows_ahead(edge_ref)
        lax.fori_loop(
            0, n, block, tuple(e[:, g * group : (g + 1) * group] for g in range(width // group))
        )
        end_out[...] = end_ref[...].astype(BF16)
        for j in range(n):
            pltpu.make_async_copy(
                buf.at[j], xc_ref.at[pl.ds(j * tok, tok), :], out_sems.at[j]
            ).wait()

    return pl.pallas_call(
        body,
        grid_spec=pltpu.PrefetchScalarGridSpec(
            num_scalar_prefetch=1,
            grid=(1,),
            in_specs=[ANY] * n
            + [
                pl.BlockSpec((SENT_ROWS, width), lambda i, me: (0, first // width)),
                pl.BlockSpec((CONV, width), lambda i, me: (0, me[0] * per + first // width)),
                pl.BlockSpec((1, width), lambda i, me: (0, me[0] * per + first // width)),
                whole(bt.shape),
                whole(wv.shape),
            ]
            + [ANY] * len(after),
            out_specs=[ANY, whole((STATE, width))],
            scratch_shapes=[
                pltpu.VMEM((n, tok, width), BF16),
                pltpu.VMEM((tok, width), F32),
                pltpu.VMEM((STATE, width), F32),
                pltpu.SemaphoreType.DMA((n,)),
                pltpu.SemaphoreType.DMA((n,)),
            ],
        ),
        out_shape=[
            jax.ShapeDtypeStruct((total, width), BF16),
            jax.ShapeDtypeStruct((STATE, width), BF16),
        ],
        compiler_params=params(),
        cost_estimate=cost(2 * total * STATE * width, 4 * total * width + 4 * total * STATE),
        name="convolve",
    )(me, x_in, *received, edge, weight, bias, bt, wv, *after)


def emit(y, xc, bt, c, m, wu, ec, ends, decays, skip, heads_dev, channels, width, first):
    total = xc.shape[0]
    tok = m.shape[1]
    group = min(width, 256)
    n_ends, n_decays = len(ends), len(decays)
    alias = [] if y is None else [y]

    def body(*refs):
        refs = refs[len(alias) :]
        xc_ref, bt_ref, c_ref, m_ref, wu_ref, ec_ref, skip_ref = refs[:7]
        end_refs, refs = refs[7 : 7 + n_ends], refs[7 + n_ends :]
        decay_refs, (out_ref, token_ref, state) = refs[:n_decays], refs[n_decays:]

        @pl.when(pl.program_id(0) == 0)
        def _():
            carried = end_refs[-1][...].astype(F32)
            for i in reversed(range(n_ends - 1)):
                d = spread(decay_refs[i][...], heads_dev, first // HEADDIM, width)[:1]
                carried = end_refs[i][...].astype(F32) + d * carried
            state[...] = carried
            token_ref[...] = jnp.zeros_like(token_ref)

        for g in range(width // group):
            cols = slice(g * group, (g + 1) * group)
            head = first // HEADDIM + g * (group // HEADDIM)
            x = xc_ref[:, cols].astype(F32)
            u = (x * spread(wu_ref[...], heads_dev, head, group)).astype(BF16)
            e = spread(ec_ref[...], heads_dev, head, group)
            s = state[:, cols]
            y_g = jnp.dot(m_ref[...], u, preferred_element_type=F32)
            y_g += jnp.dot(c_ref[...], s.astype(BF16), preferred_element_type=F32)
            out_ref[:, cols] = (e * y_g + skip_ref[:, cols] * x).astype(BF16)
            s = s + jnp.dot(bt_ref[...], u, preferred_element_type=F32)
            state[:, cols] = e[tok - 1 :] * s

    row = lambda j: (j, 0)
    return pl.pallas_call(
        body,
        grid=(total // tok,),
        in_specs=[ANY] * len(alias)
        + [
            pl.BlockSpec((tok, width), row),
            pl.BlockSpec((STATE, tok), lambda j: (0, j)),
            pl.BlockSpec((tok, STATE), row),
            pl.BlockSpec((tok, tok), row),
            pl.BlockSpec((tok, LANES), row),
            pl.BlockSpec((tok, LANES), row),
            pl.BlockSpec((1, width), lambda j: (0, first // width)),
        ]
        + [whole((STATE, width))] * n_ends
        + [whole((2 * EDGE_ROWS, LANES))] * n_decays,
        out_specs=[
            pl.BlockSpec((tok, width), lambda j: (j, first // width)),
            whole((EDGE_ROWS, LANES)),
        ],
        out_shape=[
            jax.ShapeDtypeStruct((total, channels), BF16),
            jax.ShapeDtypeStruct((EDGE_ROWS, LANES), F32),
        ],
        scratch_shapes=[pltpu.VMEM((STATE, width), F32)],
        input_output_aliases={0: 0} if alias else {},
        compiler_params=params(),
        cost_estimate=cost(6 * total * STATE * width, 4 * total * width + 6 * total * STATE),
        name="emit",
    )(*alias, xc, bt, c, m, wu, ec, skip, *ends, *decays)


def shards(
    x_in,
    bc_in,
    dt_raw,
    dt_bias,
    a_log,
    d_skip,
    conv_x_weight,
    conv_x_bias,
    conv_bc_weight,
    conv_bc_bias,
):
    n = lax.axis_size("inner")
    n_slab = lax.axis_size("slab")
    heads_dev = HEADS // n
    channels = heads_dev * HEADDIM
    per_group = HEADS // GROUPS
    index = lax.axis_index("inner")
    me = index.astype(jnp.int32).reshape(1)

    middle = n // 2
    shifts = sorted(range(1, n), key=lambda s: abs(s - middle))

    def rotate(arrays, chosen):
        for s in chosen:
            arrays[s - 1] = lax.ppermute(
                arrays[s - 1], "inner", [(i, (i + s) % n) for i in range(n)]
            )

    def forward(a, by):
        return lax.ppermute(a, "slab", [(i, i + by) for i in range(n_slab - by)])

    def mine(v):
        return lax.dynamic_slice_in_dim(v, index * heads_dev, heads_dev, 0)

    def send(k, after):
        width, first = widths[k], sum(widths[:k])
        parts = list(pack_x(me, x_in, n, channels, width, first, after))
        rotate(parts, shifts[1:2])
        rotate(parts, shifts[:1] + shifts[2:])
        return parts

    widths = chunk_widths(channels)
    packed = list(pack_bc(me, bc_in, dt_raw, n, heads_dev, per_group))
    messages = packed[1:]
    rotate(messages, shifts)
    messages = packed[:1] + messages
    received = [send(k, []) for k in range(len(widths))]
    edges = pack_edge(x_in, bc_in, n, channels, heads_dev, per_group)
    edges = [
        lax.ppermute(
            e, ("slab", "inner"), [(s * n + n - 1, (s + 1) * n + j) for s in range(n_slab - 1)]
        )
        for j, e in enumerate(edges)
    ]
    edge = sum(edges)
    skip = jnp.repeat(mine(d_skip), HEADDIM)[None, :]
    bt, c, m, wu, wv, ec, dv = prepare(
        me,
        messages,
        edge[:, channels:],
        conv_bc_weight,
        conv_bc_bias[None, :],
        mine(dt_bias)[:, None],
        mine(a_log)[:, None],
        n,
        heads_dev,
        per_group,
    )
    decays = [forward(dv, by) for by in range(1, n_slab - 1)]
    y = None
    tokens, pending = [], []

    def finish():
        k, xc, ends = pending.pop(0)
        return emit(
            y,
            xc,
            bt,
            c,
            m,
            wu,
            ec,
            ends,
            decays,
            skip,
            heads_dev,
            channels,
            widths[k],
            sum(widths[:k]),
        )

    last = len(widths) - 1
    for k, width in enumerate(widths):
        xc, end = convolve(
            me,
            x_in,
            received[k],
            edge,
            conv_x_weight,
            conv_x_bias[None, :],
            bt,
            wv,
            n,
            heads_dev,
            channels,
            width,
            sum(widths[:k]),
            decays if k == 0 else tokens[-1:],
        )
        ends = [forward(end, by) for by in range(1, n_slab)]
        pending.append((k, xc, ends))
        while pending and (len(pending) > 1 or k >= last - 1):
            y, token = finish()
            tokens.append(token)
    return y


def solution(mesh):
    tokens = P(("slab", "inner"), None)
    placed = (tokens, tokens, tokens) + (P(),) * 7

    return jax.shard_map(
        shards, mesh=mesh, in_specs=placed, out_specs=P("slab", "inner"), check_vma=False
    )
```

```python
import jax
import jax.numpy as jnp
from jax import lax
from jax.experimental import pallas as pl
from jax.experimental.pallas import tpu as pltpu
from jax.sharding import PartitionSpec as P


HEADS = 256
HEADDIM = 64
STATE = 256
GROUPS = 8
CONV = 4
LANES = 128
EDGE_ROWS = 8
SENT_ROWS = 4
SEG = 16


F32 = jnp.float32
BF16 = jnp.bfloat16
ANY = pl.BlockSpec(memory_space=pl.ANY)


def whole(shape):
    return pl.BlockSpec(shape, lambda *_: (0,) * len(shape))


def params():
    return pltpu.CompilerParams(vmem_limit_bytes=63 << 20)


def cost(flops, moved):
    return pl.CostEstimate(flops=flops, bytes_accessed=moved, transcendentals=0)


def chunk_widths(channels):
    return [channels // 4] * 4


def rows_ahead(edge_ref):
    e = edge_ref[...].astype(F32)
    return jnp.concatenate([jnp.zeros((EDGE_ROWS - SENT_ROWS, e.shape[1]), F32), e], axis=0)


def silu(x):
    half = 0.5 * x
    return half + half * jnp.tanh(half)


def conv_rows(carry, rows, weight, bias):
    ext = jnp.concatenate([carry, rows], axis=0)
    acc = bias + weight[CONV - 1 : CONV] * rows
    for back in range(1, CONV):
        shifted = pltpu.roll(ext, back, 0)[EDGE_ROWS:]
        acc = acc + weight[CONV - 1 - back : CONV - back] * shifted
    return silu(acc).astype(BF16)


def spread(per_head, first, width):
    lane = lax.broadcasted_iota(jnp.int32, per_head.shape, 1)
    parts = []
    for h in range(first, first + width // HEADDIM, LANES // HEADDIM):
        parts.append(jnp.take_along_axis(per_head, h + lane // HEADDIM, axis=1))
    return parts[0] if len(parts) == 1 else jnp.concatenate(parts, axis=1)


def pack_bc(bc_in, dt_raw, n, heads_dev, per_group):
    tok = bc_in.shape[0]

    def body(bc_ref, dt_ref, out_ref):
        turned = dt_ref[...].astype(F32).T.astype(BF16)
        for d in range(n):
            g = d * heads_dev // per_group * STATE
            out_ref[d, :tok, :STATE] = bc_ref[:, g : g + STATE]
            g += GROUPS * STATE
            out_ref[d, :tok, STATE:] = bc_ref[:, g : g + STATE]
            for seg in range(2):
                first = d * heads_dev + seg * SEG
                if seg * SEG < heads_dev:
                    part = turned[first : first + SEG]
                else:
                    part = jnp.zeros((SEG, tok), BF16)
                out_ref[d, tok:, seg * tok : (seg + 1) * tok] = part

    shape = (n, tok + SEG, 2 * STATE)
    return pl.pallas_call(
        body,
        grid=(1,),
        in_specs=[whole(bc_in.shape), whole(dt_raw.shape)],
        out_specs=whole(shape),
        out_shape=jax.ShapeDtypeStruct(shape, BF16),
        compiler_params=params(),
        cost_estimate=cost(0, 4 * bc_in.size),
        name="pack_bc",
    )(bc_in, dt_raw)


def by_permutes(k):
    return k % 2 == 0


def pack_x(me, x_in, n, channels, widths):
    tok = x_in.shape[0]
    step = min(64, tok)
    specs, shapes = [], []
    for k, width in enumerate(widths):
        if by_permutes(k):
            specs += [pl.BlockSpec((step, width), lambda i, me: (i, 0))] * (n - 1)
            shapes += [(tok, width)] * (n - 1)
        else:
            specs.append(pl.BlockSpec((n, step, width), lambda i, me: (0, i, 0)))
            shapes.append((n, tok, width))

    def body(me_ref, x_ref, *outs):
        outs, first = list(outs), 0
        for k, width in enumerate(widths):
            if by_permutes(k):
                for s in range(1, n):
                    col = ((me_ref[0] + s) % n) * channels + first
                    outs.pop(0)[...] = x_ref[:, pl.ds(pl.multiple_of(col, LANES), width)]
            else:
                out = outs.pop(0)
                for d in range(n):
                    col = d * channels + first
                    out[d] = x_ref[:, col : col + width]
            first += width

    parts = pl.pallas_call(
        body,
        grid_spec=pltpu.PrefetchScalarGridSpec(
            num_scalar_prefetch=1,
            grid=(tok // step,),
            in_specs=[pl.BlockSpec((step, n * channels), lambda i, me: (i, 0))],
            out_specs=specs,
        ),
        out_shape=[jax.ShapeDtypeStruct(shape, BF16) for shape in shapes],
        compiler_params=params(),
        cost_estimate=cost(0, 4 * tok * channels * n),
        name="pack_x",
    )(me, x_in)
    parts, sets = list(parts), []
    for k in range(len(widths)):
        count = n - 1 if by_permutes(k) else 1
        sets.append([parts.pop(0) for _ in range(count)])
    return sets


def pack_edge(x_in, bc_in, n, channels, heads_dev, per_group):
    tok = x_in.shape[0]
    wide = channels + 2 * STATE

    def body(x_ref, bc_ref, *outs):
        x = x_ref[...].astype(F32)[2 * EDGE_ROWS - SENT_ROWS :].astype(BF16)
        bc = bc_ref[...].astype(F32)[2 * EDGE_ROWS - SENT_ROWS :].astype(BF16)
        for j in range(n):
            g = j * heads_dev // per_group
            outs[j][:, :channels] = x[:, j * channels : (j + 1) * channels]
            outs[j][:, channels : channels + STATE] = bc[:, g * STATE : (g + 1) * STATE]
            g += GROUPS
            outs[j][:, channels + STATE :] = bc[:, g * STATE : (g + 1) * STATE]

    last = tok // (2 * EDGE_ROWS) - 1
    return pl.pallas_call(
        body,
        grid=(1,),
        in_specs=[
            pl.BlockSpec((2 * EDGE_ROWS, x_in.shape[1]), lambda i: (last, 0)),
            pl.BlockSpec((2 * EDGE_ROWS, bc_in.shape[1]), lambda i: (last, 0)),
        ],
        out_specs=[whole((SENT_ROWS, wide))] * n,
        out_shape=[jax.ShapeDtypeStruct((SENT_ROWS, wide), BF16)] * n,
        compiler_params=params(),
        cost_estimate=cost(0, 4 * EDGE_ROWS * wide * n),
        name="pack_edge",
    )(x_in, bc_in)


def prepare(me, message, edge, weight, bias, dt_bias, a_log, n, heads_dev, per_group):
    rows = message.shape[1]
    tok = rows - SEG
    total = n * tok

    def body(me_ref, *refs):
        msg_ref, refs = refs[0], refs[1:]
        edge_ref, wb_ref, wc_ref, bb_ref, bc_ref, dtb_ref, al_ref = refs[:7]
        bt_out, c_out, m_out, wu_out, ec_out, dj_out, pj_out, dv_out = refs[7:15]
        buf, sems = refs[15:]
        copy = pltpu.make_async_copy(msg_ref, buf, sems.at[0])
        copy.start()
        copy.wait()

        def turn(w):
            pad = jnp.zeros((LANES - heads_dev, w.shape[1]), F32)
            return jnp.concatenate([w, pad], axis=0).T

        at = lax.broadcasted_iota(jnp.int32, (tok, tok), 0)
        to = lax.broadcasted_iota(jnp.int32, (tok, tok), 1)
        upto = jnp.where(at <= to, 1.0, 0.0).astype(F32)
        rate = -jnp.exp(al_ref[...])
        ends, aheads = [], [jnp.zeros((heads_dev, 1), F32)]
        for j in range(n):
            dt_raw = buf[j, tok:, :].astype(F32)
            segs = [dt_raw[:, i * tok : (i + 1) * tok] for i in range(heads_dev // SEG)]
            dt = jax.nn.softplus(jnp.concatenate(segs, axis=0) + dtb_ref[...])
            cum = jnp.dot(
                dt * rate,
                upto,
                precision=lax.Precision.HIGHEST,
                preferred_element_type=F32,
            )
            here = pl.ds(j * tok, tok)
            wu_out[here, :] = turn(dt * jnp.exp(-cum))
            ec_out[here, :] = turn(jnp.exp(cum))
            ends.append(cum[:, tok - 1 :])
            aheads.append(aheads[-1] + ends[-1])
        pad = jnp.zeros((heads_dev, LANES - n), F32)
        dj_out[...] = turn(jnp.exp(jnp.concatenate(ends + [pad], axis=1)))
        pj_out[...] = turn(jnp.exp(jnp.concatenate(aheads[:-1] + [pad], axis=1)))
        decay = jnp.broadcast_to(jnp.exp(aheads[-1]), (heads_dev, LANES))
        dv_out[...] = turn(decay)[: dv_out.shape[0]]

        strip = 32
        lower = at >= to

        def block(j, carry):
            def step(i, carry):
                r = pl.multiple_of(i * strip, strip)
                x = buf[j, pl.ds(r, strip), :].astype(F32)
                new = []
                for half, w_ref, b_ref in ((0, wb_ref, bb_ref), (1, wc_ref, bc_ref)):
                    mine = x[:, half * STATE : (half + 1) * STATE]
                    done = conv_rows(carry[half], mine, w_ref[...], b_ref[...])
                    buf[j, pl.ds(r, strip), half * STATE : (half + 1) * STATE] = done
                    new.append(mine[strip - EDGE_ROWS :])
                return tuple(new)

            carry = lax.fori_loop(0, tok // strip, step, carry)
            b, c = buf[j, :tok, :STATE], buf[j, :tok, STATE:]
            t = pl.multiple_of(j * tok, tok)
            turned = b.astype(F32).T.astype(BF16)
            bt_out[:, pl.ds(t, tok)] = turned
            c_out[pl.ds(t, tok), :] = c
            scores = jnp.dot(c, turned, preferred_element_type=F32)
            m_out[pl.ds(t, tok), :] = jnp.where(lower, scores, 0.0).astype(BF16)
            return carry

        e = rows_ahead(edge_ref)
        lax.fori_loop(0, n, block, (e[:, :STATE], e[:, STATE:]))

    def group(base):
        return lambda i, me: (0, base + me[0] * heads_dev // per_group)

    vec = (heads_dev, 1)
    shapes = [(STATE, total), (total, STATE), (total, tok)]
    wide = [(total, LANES), (total, LANES), (LANES, LANES), (LANES, LANES), (EDGE_ROWS, LANES)]
    return pl.pallas_call(
        body,
        grid_spec=pltpu.PrefetchScalarGridSpec(
            num_scalar_prefetch=1,
            grid=(1,),
            in_specs=[ANY]
            + [
                whole(edge.shape),
                pl.BlockSpec((CONV, STATE), group(0)),
                pl.BlockSpec((CONV, STATE), group(GROUPS)),
                pl.BlockSpec((1, STATE), group(0)),
                pl.BlockSpec((1, STATE), group(GROUPS)),
                whole(vec),
                whole(vec),
            ],
            out_specs=[whole(s) for s in shapes + wide],
            scratch_shapes=[
                pltpu.VMEM((n, rows, 2 * STATE), BF16),
                pltpu.SemaphoreType.DMA((1,)),
            ],
        ),
        out_shape=[jax.ShapeDtypeStruct(s, BF16) for s in shapes]
        + [jax.ShapeDtypeStruct(s, F32) for s in wide],
        compiler_params=params(),
        cost_estimate=cost(4 * total * STATE * tok, 20 * total * STATE),
        name="prepare",
    )(me, message, edge, weight, weight, bias, bias, dt_bias, a_log)


def convolve(me, x_in, received, edge, weight, bias, bt, wu, dj, n, channels, width, first, after):
    tok = x_in.shape[0]
    total = n * tok
    got_count = len(received)
    group = min(width, 256)
    strip = 64
    lead = 2 * EDGE_ROWS

    def body(me_ref, x_ref, *refs):
        got, refs = refs[:got_count], refs[got_count:]
        edge_ref, w_ref, b_ref, bt_ref, wu_ref, dj_ref = refs[:6]
        xc_ref, u_ref, s_ref, end_out = refs[6 + len(after) : 10 + len(after)]
        x_buf, xf_buf, xc_buf, u_buf, s_buf, state, decs, sems, out_sems = refs[
            10 + len(after) :
        ]

        def slot(j):
            return x_buf.at[pl.ds(pl.multiple_of(j * tok, tok), tok), :]

        for s in range(n):
            if got_count == 1:
                j, src = s, got[0].at[s]
            else:
                j = lax.rem(me_ref[0] - s + n, n)
                if s:
                    src = got[s - 1]
                else:
                    col = pl.multiple_of(me_ref[0] * channels + first, LANES)
                    src = x_ref.at[:, pl.ds(col, width)]
            pltpu.make_async_copy(src, slot(j), sems.at[j]).start()
        decs[...] = spread(dj_ref[: decs.shape[0], :], first // HEADDIM, width)
        e = rows_ahead(edge_ref)
        for g in range(width // LANES):
            xf_buf[g, EDGE_ROWS:lead, :] = e[:, g * LANES : (g + 1) * LANES]
        state[...] = jnp.zeros_like(state)

        def outgoing(j):
            t = pl.multiple_of(j * tok, tok)
            q = pl.multiple_of(j * STATE, STATE)
            return (
                pltpu.make_async_copy(
                    xc_buf.at[pl.ds(t, tok), :], xc_ref.at[pl.ds(t, tok), :], out_sems.at[0, j]
                ),
                pltpu.make_async_copy(
                    u_buf.at[pl.ds(t, tok), :], u_ref.at[pl.ds(t, tok), :], out_sems.at[1, j]
                ),
                pltpu.make_async_copy(
                    s_buf.at[pl.ds(q, STATE), :], s_ref.at[pl.ds(q, STATE), :], out_sems.at[2, j]
                ),
            )

        def block(j, carry):
            pltpu.make_async_copy(slot(j), slot(j), sems.at[j]).wait()
            t = pl.multiple_of(j * tok, tok)
            q = pl.multiple_of(j * STATE, STATE)
            for i in range(tok // strip):
                r = pl.multiple_of(t + i * strip, strip)
                per_head = wu_ref[pl.ds(r, strip), :]
                for g in range(width // LANES):
                    cols = slice(g * LANES, (g + 1) * LANES)
                    low = lead + i * strip
                    x = x_buf[pl.ds(r, strip), cols].astype(F32)
                    xf_buf[g, low : low + strip, :] = x
                    acc = b_ref[:, cols] + w_ref[CONV - 1 :, cols] * x
                    for back in range(1, CONV):
                        acc = acc + (
                            w_ref[CONV - 1 - back : CONV - back, cols]
                            * xf_buf[g, low - back : low - back + strip, :]
                        )
                    xc = silu(acc).astype(BF16)
                    xc_buf[pl.ds(r, strip), cols] = xc
                    scale = spread(per_head, (first + g * LANES) // HEADDIM, LANES)
                    u_buf[pl.ds(r, strip), cols] = (xc.astype(F32) * scale).astype(BF16)
            for g in range(width // LANES):
                xf_buf[g, EDGE_ROWS:lead, :] = xf_buf[g, lead + tok - EDGE_ROWS : lead + tok, :]
            lhs = bt_ref[:, pl.ds(t, tok)]
            for g in range(width // group):
                cols = slice(g * group, (g + 1) * group)
                old = state[:, cols]
                s_buf[pl.ds(q, STATE), cols] = old.astype(BF16)
                added = jnp.dot(lhs, u_buf[pl.ds(t, tok), cols], preferred_element_type=F32)
                state[:, cols] = decs[pl.ds(j, 1), cols] * (old + added)
            for copy in outgoing(j):
                copy.start()
            return carry

        lax.fori_loop(0, n, block, 0)
        end_out[...] = state[...].astype(BF16)
        for j in range(n):
            for copy in outgoing(j):
                copy.wait()

    def columns(rows):
        per = channels // width if channels % width == 0 and first % width == 0 else 0
        if per:
            return pl.BlockSpec((rows, width), lambda i, me: (0, me[0] * per + first // width))
        return pl.BlockSpec(
            (pl.Element(rows), pl.Element(width)),
            lambda i, me: (0, pl.multiple_of(me[0] * channels + first, LANES)),
        )

    return pl.pallas_call(
        body,
        grid_spec=pltpu.PrefetchScalarGridSpec(
            num_scalar_prefetch=1,
            grid=(1,),
            in_specs=[ANY] * (1 + got_count)
            + [
                whole((SENT_ROWS, width)),
                columns(CONV),
                columns(1),
                whole(bt.shape),
                whole(wu.shape),
                whole(dj.shape),
            ]
            + [ANY] * len(after),
            out_specs=[ANY, ANY, ANY, whole((STATE, width))],
            scratch_shapes=[
                pltpu.VMEM((total, width), BF16),
                pltpu.VMEM((width // LANES, lead + tok, LANES), F32),
                pltpu.VMEM((total, width), BF16),
                pltpu.VMEM((total, width), BF16),
                pltpu.VMEM((n * STATE, width), BF16),
                pltpu.VMEM((STATE, width), F32),
                pltpu.VMEM((-(-n // EDGE_ROWS) * EDGE_ROWS, width), F32),
                pltpu.SemaphoreType.DMA((n,)),
                pltpu.SemaphoreType.DMA((3, n)),
            ],
        ),
        out_shape=[
            jax.ShapeDtypeStruct((total, width), BF16),
            jax.ShapeDtypeStruct((total, width), BF16),
            jax.ShapeDtypeStruct((n * STATE, width), BF16),
            jax.ShapeDtypeStruct((STATE, width), BF16),
        ],
        compiler_params=params(),
        cost_estimate=cost(2 * total * STATE * width, 6 * total * width + 4 * total * STATE),
        name="convolve",
    )(me, x_in, *received, edge, weight, bias, bt, wu, dj, *after)


def emit(y, xc, u, s_loc, c, m, ec, pj, ends, decays, skip, channels, width, first):
    total = xc.shape[0]
    tok = m.shape[1]
    group = min(width, 256)
    n_ends, n_decays = len(ends), len(decays)
    alias = [] if y is None else [y]
    fold = 2

    def body(*refs):
        refs = refs[len(alias) :]
        xc_ref, u_ref, s_ref, c_ref, m_ref, ec_ref, pj_ref, skip_ref = refs[:8]
        end_refs, refs = refs[8 : 8 + n_ends], refs[8 + n_ends :]
        decay_refs, (out_ref, token_ref, carry, steps) = refs[:n_decays], refs[n_decays:]

        @pl.when(pl.program_id(0) == 0)
        def _():
            steps[...] = spread(pj_ref[: steps.shape[0], :], first // HEADDIM, width)
            carried = end_refs[-1][...].astype(F32)
            for i in reversed(range(n_ends - 1)):
                d = spread(decay_refs[i][...], first // HEADDIM, width)[:1]
                carried = end_refs[i][...].astype(F32) + d * carried
            carry[...] = carried
            token_ref[...] = jnp.zeros_like(token_ref)

        for b in range(fold):
            step = steps[pl.ds(pl.program_id(0) * fold + b, 1), :]
            rows = slice(b * tok, (b + 1) * tok)
            states = slice(b * STATE, (b + 1) * STATE)
            for g in range(width // group):
                cols = slice(g * group, (g + 1) * group)
                s = s_ref[states, cols].astype(F32) + step[:, cols] * carry[:, cols]
                acc = jnp.dot(m_ref[rows, :], u_ref[rows, cols], preferred_element_type=F32)
                acc += jnp.dot(c_ref[rows, :], s.astype(BF16), preferred_element_type=F32)
                e = spread(ec_ref[rows, :], (first + g * group) // HEADDIM, group)
                x = xc_ref[rows, cols].astype(F32)
                out_ref[rows, cols] = (e * acc + skip_ref[:, cols] * x).astype(BF16)

    def ahead(shape):
        return pl.BlockSpec((fold * shape[0], shape[1]), lambda j: (j, 0))

    if channels % width == 0 and first % width == 0:
        out_spec = pl.BlockSpec((fold * tok, width), lambda j: (j, first // width))
    else:
        out_spec = pl.BlockSpec(
            (pl.Element(fold * tok), pl.Element(width)), lambda j: (j * fold * tok, first)
        )
    return pl.pallas_call(
        body,
        grid=(total // (fold * tok),),
        in_specs=[ANY] * len(alias)
        + [
            ahead((tok, width)),
            ahead((tok, width)),
            ahead((STATE, width)),
            ahead((tok, STATE)),
            ahead((tok, tok)),
            ahead((tok, LANES)),
            whole(pj.shape),
            whole((1, width)),
        ]
        + [whole((STATE, width))] * n_ends
        + [whole((EDGE_ROWS, LANES))] * n_decays,
        out_specs=[out_spec, whole((EDGE_ROWS, LANES))],
        out_shape=[
            jax.ShapeDtypeStruct((total, channels), BF16),
            jax.ShapeDtypeStruct((EDGE_ROWS, LANES), F32),
        ],
        scratch_shapes=[
            pltpu.VMEM((STATE, width), F32),
            pltpu.VMEM((-(-total // tok // EDGE_ROWS) * EDGE_ROWS, width), F32),
        ],
        input_output_aliases={0: 0} if alias else {},
        compiler_params=params(),
        cost_estimate=cost(6 * total * STATE * width, 8 * total * width + 6 * total * STATE),
        name="emit",
    )(*alias, xc, u, s_loc, c, m, ec, pj, skip, *ends, *decays)


def shards(
    x_in,
    bc_in,
    dt_raw,
    dt_bias,
    a_log,
    d_skip,
    conv_x_weight,
    conv_x_bias,
    conv_bc_weight,
    conv_bc_bias,
):
    n = lax.axis_size("inner")
    n_slab = lax.axis_size("slab")
    heads_dev = HEADS // n
    channels = heads_dev * HEADDIM
    per_group = HEADS // GROUPS
    index = lax.axis_index("inner")
    me = index.astype(jnp.int32).reshape(1)

    middle = n // 2
    shifts = sorted(range(1, n), key=lambda s: abs(s - middle))

    def rotate(arrays, chosen):
        for s in chosen:
            arrays[s - 1] = lax.ppermute(
                arrays[s - 1], "inner", [(i, (i + s) % n) for i in range(n)]
            )

    def forward(a, by):
        return lax.ppermute(a, "slab", [(i, i + by) for i in range(n_slab - by)])

    def mine(v):
        return lax.dynamic_slice_in_dim(v, index * heads_dev, heads_dev, 0)

    def exchange(a):
        return lax.all_to_all(a, "inner", split_axis=0, concat_axis=0, tiled=True)

    def send(k, parts):
        if not by_permutes(k):
            return [exchange(parts[0])]
        rotate(parts, shifts)
        return parts

    widths = chunk_widths(channels)
    packed = pack_bc(bc_in, dt_raw, n, heads_dev, per_group)
    message = exchange(packed)
    packed_x = pack_x(me, x_in, n, channels, widths)
    received = [send(k, parts) for k, parts in enumerate(packed_x)]
    edges = pack_edge(x_in, bc_in, n, channels, heads_dev, per_group)
    edges = [
        lax.ppermute(
            e, ("slab", "inner"), [(s * n + n - 1, (s + 1) * n + j) for s in range(n_slab - 1)]
        )
        for j, e in enumerate(edges)
    ]
    edge = sum(edges)
    skip = jnp.repeat(mine(d_skip), HEADDIM)[None, :]
    bt, c, m, wu, ec, dj, pj, dv = prepare(
        me,
        message,
        edge[:, channels:],
        conv_bc_weight,
        conv_bc_bias[None, :],
        mine(dt_bias)[:, None],
        mine(a_log)[:, None],
        n,
        heads_dev,
        per_group,
    )
    decays = [forward(dv, by) for by in range(1, n_slab - 1)]
    y = None
    tokens, pending = [], []

    def finish():
        k, xc, u, s_loc, ends = pending.pop(0)
        cut = slice(sum(widths[:k]), sum(widths[: k + 1]))
        return emit(
            y,
            xc,
            u,
            s_loc,
            c,
            m,
            ec,
            pj,
            ends,
            decays,
            skip[:, cut],
            channels,
            widths[k],
            cut.start,
        )

    last = len(widths) - 1
    for k, width in enumerate(widths):
        first = sum(widths[:k])
        xc, u, s_loc, end = convolve(
            me,
            x_in,
            received[k],
            edge[:, first : first + width],
            conv_x_weight,
            conv_x_bias[None, :],
            bt,
            wu,
            dj,
            n,
            channels,
            width,
            first,
            decays if k == 0 else tokens[-1:],
        )
        ends = [forward(end, by) for by in range(1, n_slab)]
        pending.append((k, xc, u, s_loc, ends))
        while pending and (len(pending) > 1 or k >= last - 1):
            y, token = finish()
            tokens.append(token)
    return y


def solution(mesh):
    tokens = P(("slab", "inner"), None)
    placed = (tokens, tokens, tokens) + (P(),) * 7

    return jax.shard_map(
        shards, mesh=mesh, in_specs=placed, out_specs=P("slab", "inner"), check_vma=False
    )
```

```python
import jax
import jax.numpy as jnp
from jax import lax
from jax.experimental import pallas as pl
from jax.experimental.pallas import tpu as pltpu
from jax.sharding import PartitionSpec as P


HEADS = 256
HEADDIM = 64
STATE = 256
GROUPS = 8
CONV = 4
LANES = 128
EDGE_ROWS = 8
SENT_ROWS = 4
SEG = 16


F32 = jnp.float32
BF16 = jnp.bfloat16
ANY = pl.BlockSpec(memory_space=pl.ANY)


def whole(shape):
    return pl.BlockSpec(shape, lambda *_: (0,) * len(shape))


def params():
    return pltpu.CompilerParams(vmem_limit_bytes=63 << 20)


def cost(flops, moved):
    return pl.CostEstimate(flops=flops, bytes_accessed=moved, transcendentals=0)


def chunk_widths(channels):
    return [channels // 8 * part for part in (2, 2, 2, 2)]


def group_width(width):
    return 256 if width % 256 == 0 else LANES


def rows_ahead(edge_ref):
    e = edge_ref[...].astype(F32)
    return jnp.concatenate([jnp.zeros((EDGE_ROWS - SENT_ROWS, e.shape[1]), F32), e], axis=0)


def silu(x):
    half = 0.5 * x
    return half + half * jnp.tanh(half)


def conv_rows(carry, rows, weight, bias):
    ext = jnp.concatenate([carry, rows], axis=0)
    acc = bias + weight[CONV - 1 : CONV] * rows
    for back in range(1, CONV):
        shifted = pltpu.roll(ext, back, 0)[EDGE_ROWS:]
        acc = acc + weight[CONV - 1 - back : CONV - back] * shifted
    return silu(acc).astype(BF16)


def spread(per_head, first, width):
    lane = lax.broadcasted_iota(jnp.int32, per_head.shape, 1)
    parts = []
    for h in range(first, first + width // HEADDIM, LANES // HEADDIM):
        parts.append(jnp.take_along_axis(per_head, h + lane // HEADDIM, axis=1))
    return parts[0] if len(parts) == 1 else jnp.concatenate(parts, axis=1)


def pack_bc(bc_in, dt_raw, n, heads_dev, per_group):
    tok = bc_in.shape[0]

    def body(bc_ref, dt_ref, out_ref):
        turned = dt_ref[...].astype(F32).T.astype(BF16)
        for d in range(n):
            g = d * heads_dev // per_group * STATE
            out_ref[d, :tok, :STATE] = bc_ref[:, g : g + STATE]
            g += GROUPS * STATE
            out_ref[d, :tok, STATE:] = bc_ref[:, g : g + STATE]
            for seg in range(2):
                first = d * heads_dev + seg * SEG
                if seg * SEG < heads_dev:
                    part = turned[first : first + SEG]
                else:
                    part = jnp.zeros((SEG, tok), BF16)
                out_ref[d, tok:, seg * tok : (seg + 1) * tok] = part

    shape = (n, tok + SEG, 2 * STATE)
    return pl.pallas_call(
        body,
        grid=(1,),
        in_specs=[whole(bc_in.shape), whole(dt_raw.shape)],
        out_specs=whole(shape),
        out_shape=jax.ShapeDtypeStruct(shape, BF16),
        compiler_params=params(),
        cost_estimate=cost(0, 4 * bc_in.size),
        name="pack_bc",
    )(bc_in, dt_raw)


def by_permutes(k):
    return k != 2


def pack_x(me, x_in, n, channels, widths):
    tok = x_in.shape[0]
    step = min(64, tok)
    specs, shapes = [], []
    for k, width in enumerate(widths):
        if by_permutes(k):
            specs += [pl.BlockSpec((step, width), lambda i, me: (i, 0))] * (n - 1)
            shapes += [(tok, width)] * (n - 1)
        else:
            specs.append(pl.BlockSpec((n, step, width), lambda i, me: (0, i, 0)))
            shapes.append((n, tok, width))

    def body(me_ref, x_ref, *outs):
        outs, first = list(outs), 0
        for k, width in enumerate(widths):
            if by_permutes(k):
                for s in range(1, n):
                    col = ((me_ref[0] + s) % n) * channels + first
                    outs.pop(0)[...] = x_ref[:, pl.ds(pl.multiple_of(col, LANES), width)]
            else:
                out = outs.pop(0)
                for d in range(n):
                    col = d * channels + first
                    out[d] = x_ref[:, col : col + width]
            first += width

    parts = pl.pallas_call(
        body,
        grid_spec=pltpu.PrefetchScalarGridSpec(
            num_scalar_prefetch=1,
            grid=(tok // step,),
            in_specs=[pl.BlockSpec((step, n * channels), lambda i, me: (i, 0))],
            out_specs=specs,
        ),
        out_shape=[jax.ShapeDtypeStruct(shape, BF16) for shape in shapes],
        compiler_params=params(),
        cost_estimate=cost(0, 4 * tok * channels * n),
        name="pack_x",
    )(me, x_in)
    parts, sets = list(parts), []
    for k in range(len(widths)):
        count = n - 1 if by_permutes(k) else 1
        sets.append([parts.pop(0) for _ in range(count)])
    return sets


def pack_edge(x_in, bc_in, n, channels, heads_dev, per_group):
    tok = x_in.shape[0]
    wide = channels + 2 * STATE

    def body(x_ref, bc_ref, *outs):
        x = x_ref[...].astype(F32)[2 * EDGE_ROWS - SENT_ROWS :].astype(BF16)
        bc = bc_ref[...].astype(F32)[2 * EDGE_ROWS - SENT_ROWS :].astype(BF16)
        for j in range(n):
            g = j * heads_dev // per_group
            outs[j][:, :channels] = x[:, j * channels : (j + 1) * channels]
            outs[j][:, channels : channels + STATE] = bc[:, g * STATE : (g + 1) * STATE]
            g += GROUPS
            outs[j][:, channels + STATE :] = bc[:, g * STATE : (g + 1) * STATE]

    last = tok // (2 * EDGE_ROWS) - 1
    return pl.pallas_call(
        body,
        grid=(1,),
        in_specs=[
            pl.BlockSpec((2 * EDGE_ROWS, x_in.shape[1]), lambda i: (last, 0)),
            pl.BlockSpec((2 * EDGE_ROWS, bc_in.shape[1]), lambda i: (last, 0)),
        ],
        out_specs=[whole((SENT_ROWS, wide))] * n,
        out_shape=[jax.ShapeDtypeStruct((SENT_ROWS, wide), BF16)] * n,
        compiler_params=params(),
        cost_estimate=cost(0, 4 * EDGE_ROWS * wide * n),
        name="pack_edge",
    )(x_in, bc_in)


def prepare(me, message, edge, weight, bias, dt_bias, a_log, n, heads_dev, per_group):
    rows = message.shape[1]
    tok = rows - SEG
    total = n * tok

    def body(me_ref, *refs):
        msg_ref, refs = refs[0], refs[1:]
        edge_ref, wb_ref, wc_ref, bb_ref, bc_ref, dtb_ref, al_ref = refs[:7]
        bt_out, c_out, m_out, wu_out, ec_out, dj_out, pj_out, dv_out = refs[7:15]
        buf, sems = refs[15:]
        copy = pltpu.make_async_copy(msg_ref, buf, sems.at[0])
        copy.start()
        copy.wait()

        def turn(w):
            pad = jnp.zeros((LANES - heads_dev, w.shape[1]), F32)
            return jnp.concatenate([w, pad], axis=0).T

        at = lax.broadcasted_iota(jnp.int32, (tok, tok), 0)
        to = lax.broadcasted_iota(jnp.int32, (tok, tok), 1)
        upto = jnp.where(at <= to, 1.0, 0.0).astype(F32)
        rate = -jnp.exp(al_ref[...])
        ends, aheads = [], [jnp.zeros((heads_dev, 1), F32)]
        for j in range(n):
            dt_raw = buf[j, tok:, :].astype(F32)
            segs = [dt_raw[:, i * tok : (i + 1) * tok] for i in range(heads_dev // SEG)]
            dt = jax.nn.softplus(jnp.concatenate(segs, axis=0) + dtb_ref[...])
            cum = jnp.dot(
                dt * rate,
                upto,
                precision=lax.Precision.HIGHEST,
                preferred_element_type=F32,
            )
            here = pl.ds(j * tok, tok)
            wu_out[here, :] = turn(dt * jnp.exp(-cum))
            ec_out[here, :] = turn(jnp.exp(cum))
            ends.append(cum[:, tok - 1 :])
            aheads.append(aheads[-1] + ends[-1])
        pad = jnp.zeros((heads_dev, LANES - n), F32)
        dj_out[...] = turn(jnp.exp(jnp.concatenate(ends + [pad], axis=1)))
        pj_out[...] = turn(jnp.exp(jnp.concatenate(aheads[:-1] + [pad], axis=1)))
        decay = jnp.broadcast_to(jnp.exp(aheads[-1]), (heads_dev, LANES))
        dv_out[...] = turn(decay)[: dv_out.shape[0]]

        strip = 32
        lower = at >= to

        def block(j, carry):
            def step(i, carry):
                r = pl.multiple_of(i * strip, strip)
                x = buf[j, pl.ds(r, strip), :].astype(F32)
                new = []
                for half, w_ref, b_ref in ((0, wb_ref, bb_ref), (1, wc_ref, bc_ref)):
                    mine = x[:, half * STATE : (half + 1) * STATE]
                    done = conv_rows(carry[half], mine, w_ref[...], b_ref[...])
                    buf[j, pl.ds(r, strip), half * STATE : (half + 1) * STATE] = done
                    new.append(mine[strip - EDGE_ROWS :])
                return tuple(new)

            carry = lax.fori_loop(0, tok // strip, step, carry)
            b, c = buf[j, :tok, :STATE], buf[j, :tok, STATE:]
            t = pl.multiple_of(j * tok, tok)
            turned = b.astype(F32).T.astype(BF16)
            bt_out[:, pl.ds(t, tok)] = turned
            c_out[pl.ds(t, tok), :] = c
            scores = jnp.dot(c, turned, preferred_element_type=F32)
            m_out[pl.ds(t, tok), :] = jnp.where(lower, scores, 0.0).astype(BF16)
            return carry

        e = rows_ahead(edge_ref)
        lax.fori_loop(0, n, block, (e[:, :STATE], e[:, STATE:]))

    def group(base):
        return lambda i, me: (0, base + me[0] * heads_dev // per_group)

    vec = (heads_dev, 1)
    shapes = [(STATE, total), (total, STATE), (total, tok)]
    wide = [(total, LANES), (total, LANES), (LANES, LANES), (LANES, LANES), (EDGE_ROWS, LANES)]
    return pl.pallas_call(
        body,
        grid_spec=pltpu.PrefetchScalarGridSpec(
            num_scalar_prefetch=1,
            grid=(1,),
            in_specs=[ANY]
            + [
                whole(edge.shape),
                pl.BlockSpec((CONV, STATE), group(0)),
                pl.BlockSpec((CONV, STATE), group(GROUPS)),
                pl.BlockSpec((1, STATE), group(0)),
                pl.BlockSpec((1, STATE), group(GROUPS)),
                whole(vec),
                whole(vec),
            ],
            out_specs=[whole(s) for s in shapes + wide],
            scratch_shapes=[
                pltpu.VMEM((n, rows, 2 * STATE), BF16),
                pltpu.SemaphoreType.DMA((1,)),
            ],
        ),
        out_shape=[jax.ShapeDtypeStruct(s, BF16) for s in shapes]
        + [jax.ShapeDtypeStruct(s, F32) for s in wide],
        compiler_params=params(),
        cost_estimate=cost(4 * total * STATE * tok, 20 * total * STATE),
        name="prepare",
    )(me, message, edge, weight, weight, bias, bias, dt_bias, a_log)


def convolve(me, x_in, received, edge, weight, bias, bt, wu, dj, n, channels, width, first, after):
    tok = x_in.shape[0]
    total = n * tok
    got_count = len(received)
    group = group_width(width)
    strip = 64
    lead = 2 * EDGE_ROWS

    def body(me_ref, x_ref, *refs):
        got, refs = refs[:got_count], refs[got_count:]
        edge_ref, w_ref, b_ref, bt_ref, wu_ref, dj_ref = refs[:6]
        xc_ref, u_ref, s_ref, end_out = refs[6 + len(after) : 10 + len(after)]
        x_buf, xf_buf, xc_buf, u_buf, s_buf, state, decs, sems, out_sems = refs[
            10 + len(after) :
        ]

        def slot(j):
            return x_buf.at[pl.ds(pl.multiple_of(j * tok, tok), tok), :]

        for s in range(n):
            if got_count == 1:
                j, src = s, got[0].at[s]
            else:
                j = lax.rem(me_ref[0] - s + n, n)
                if s:
                    src = got[s - 1]
                else:
                    col = pl.multiple_of(me_ref[0] * channels + first, LANES)
                    src = x_ref.at[:, pl.ds(col, width)]
            pltpu.make_async_copy(src, slot(j), sems.at[j]).start()
        decs[...] = spread(dj_ref[: decs.shape[0], :], first // HEADDIM, width)
        e = rows_ahead(edge_ref)
        for g in range(width // LANES):
            xf_buf[g, EDGE_ROWS:lead, :] = e[:, first + g * LANES : first + (g + 1) * LANES]
        state[...] = jnp.zeros_like(state)

        def outgoing(j):
            t = pl.multiple_of(j * tok, tok)
            q = pl.multiple_of(j * STATE, STATE)
            return (
                pltpu.make_async_copy(
                    xc_buf.at[pl.ds(t, tok), :], xc_ref.at[pl.ds(t, tok), :], out_sems.at[0, j]
                ),
                pltpu.make_async_copy(
                    u_buf.at[pl.ds(t, tok), :], u_ref.at[pl.ds(t, tok), :], out_sems.at[1, j]
                ),
                pltpu.make_async_copy(
                    s_buf.at[pl.ds(q, STATE), :], s_ref.at[pl.ds(q, STATE), :], out_sems.at[2, j]
                ),
            )

        def block(j, carry):
            pltpu.make_async_copy(slot(j), slot(j), sems.at[j]).wait()
            t = pl.multiple_of(j * tok, tok)
            q = pl.multiple_of(j * STATE, STATE)
            for i in range(tok // strip):
                r = pl.multiple_of(t + i * strip, strip)
                per_head = wu_ref[pl.ds(r, strip), :]
                for g in range(width // LANES):
                    cols = slice(g * LANES, (g + 1) * LANES)
                    here = slice(first + g * LANES, first + (g + 1) * LANES)
                    low = lead + i * strip
                    x = x_buf[pl.ds(r, strip), cols].astype(F32)
                    xf_buf[g, low : low + strip, :] = x
                    acc = b_ref[:, here] + w_ref[CONV - 1 :, here] * x
                    for back in range(1, CONV):
                        acc = acc + (
                            w_ref[CONV - 1 - back : CONV - back, here]
                            * xf_buf[g, low - back : low - back + strip, :]
                        )
                    xc = silu(acc).astype(BF16)
                    xc_buf[pl.ds(r, strip), cols] = xc
                    scale = spread(per_head, (first + g * LANES) // HEADDIM, LANES)
                    u_buf[pl.ds(r, strip), cols] = (xc.astype(F32) * scale).astype(BF16)
            for g in range(width // LANES):
                xf_buf[g, EDGE_ROWS:lead, :] = xf_buf[g, lead + tok - EDGE_ROWS : lead + tok, :]
            lhs = bt_ref[:, pl.ds(t, tok)]
            for g in range(width // group):
                cols = slice(g * group, (g + 1) * group)
                old = state[:, cols]
                s_buf[pl.ds(q, STATE), cols] = old.astype(BF16)
                added = jnp.dot(lhs, u_buf[pl.ds(t, tok), cols], preferred_element_type=F32)
                state[:, cols] = decs[pl.ds(j, 1), cols] * (old + added)
            for copy in outgoing(j):
                copy.start()
            return carry

        lax.fori_loop(0, n, block, 0)
        end_out[...] = state[...].astype(BF16)
        for j in range(n):
            for copy in outgoing(j):
                copy.wait()

    return pl.pallas_call(
        body,
        grid_spec=pltpu.PrefetchScalarGridSpec(
            num_scalar_prefetch=1,
            grid=(1,),
            in_specs=[ANY] * (1 + got_count)
            + [
                whole(edge.shape),
                whole(weight.shape),
                whole(bias.shape),
                whole(bt.shape),
                whole(wu.shape),
                whole(dj.shape),
            ]
            + [ANY] * len(after),
            out_specs=[ANY, ANY, ANY, whole((STATE, width))],
            scratch_shapes=[
                pltpu.VMEM((total, width), BF16),
                pltpu.VMEM((width // LANES, lead + tok, LANES), F32),
                pltpu.VMEM((total, width), BF16),
                pltpu.VMEM((total, width), BF16),
                pltpu.VMEM((n * STATE, width), BF16),
                pltpu.VMEM((STATE, width), F32),
                pltpu.VMEM((-(-n // EDGE_ROWS) * EDGE_ROWS, width), F32),
                pltpu.SemaphoreType.DMA((n,)),
                pltpu.SemaphoreType.DMA((3, n)),
            ],
        ),
        out_shape=[
            jax.ShapeDtypeStruct((total, width), BF16),
            jax.ShapeDtypeStruct((total, width), BF16),
            jax.ShapeDtypeStruct((n * STATE, width), BF16),
            jax.ShapeDtypeStruct((STATE, width), BF16),
        ],
        compiler_params=params(),
        cost_estimate=cost(2 * total * STATE * width, 6 * total * width + 4 * total * STATE),
        name="convolve",
    )(me, x_in, *received, edge, weight, bias, bt, wu, dj, *after)


def emit(y, xc, u, s_loc, c, m, ec, pj, ends, decays, skip, channels, width, first):
    total = xc.shape[0]
    tok = m.shape[1]
    group = group_width(width)
    n_ends, n_decays = len(ends), len(decays)
    alias = [] if y is None else [y]
    fold = 4

    def body(*refs):
        refs = refs[len(alias) :]
        xc_ref, u_ref, s_ref, c_ref, m_ref, ec_ref, pj_ref, skip_ref = refs[:8]
        end_refs, refs = refs[8 : 8 + n_ends], refs[8 + n_ends :]
        decay_refs, (out_ref, token_ref, carry, steps) = refs[:n_decays], refs[n_decays:]

        @pl.when(pl.program_id(0) == 0)
        def _():
            steps[...] = spread(pj_ref[: steps.shape[0], :], first // HEADDIM, width)
            carried = end_refs[-1][...].astype(F32)
            for i in reversed(range(n_ends - 1)):
                d = spread(decay_refs[i][...], first // HEADDIM, width)[:1]
                carried = end_refs[i][...].astype(F32) + d * carried
            carry[...] = carried
            token_ref[...] = jnp.zeros_like(token_ref)

        for b in range(fold):
            step = steps[pl.ds(pl.program_id(0) * fold + b, 1), :]
            rows = slice(b * tok, (b + 1) * tok)
            states = slice(b * STATE, (b + 1) * STATE)
            for g in range(width // group):
                cols = slice(g * group, (g + 1) * group)
                s = s_ref[states, cols].astype(F32) + step[:, cols] * carry[:, cols]
                acc = jnp.dot(m_ref[rows, :], u_ref[rows, cols], preferred_element_type=F32)
                acc += jnp.dot(c_ref[rows, :], s.astype(BF16), preferred_element_type=F32)
                e = spread(ec_ref[rows, :], (first + g * group) // HEADDIM, group)
                x = xc_ref[rows, cols].astype(F32)
                here = slice(first + g * group, first + (g + 1) * group)
                out_ref[rows, cols] = (e * acc + skip_ref[:, here] * x).astype(BF16)

    def ahead(shape):
        return pl.BlockSpec((fold * shape[0], shape[1]), lambda j: (j, 0))

    if channels % width == 0 and first % width == 0:
        out_spec = pl.BlockSpec((fold * tok, width), lambda j: (j, first // width))
    else:
        out_spec = pl.BlockSpec(
            (pl.Element(fold * tok), pl.Element(width)), lambda j: (j * fold * tok, first)
        )
    return pl.pallas_call(
        body,
        grid=(total // (fold * tok),),
        in_specs=[ANY] * len(alias)
        + [
            ahead((tok, width)),
            ahead((tok, width)),
            ahead((STATE, width)),
            ahead((tok, STATE)),
            ahead((tok, tok)),
            ahead((tok, LANES)),
            whole(pj.shape),
            whole(skip.shape),
        ]
        + [whole((STATE, width))] * n_ends
        + [whole((EDGE_ROWS, LANES))] * n_decays,
        out_specs=[out_spec, whole((EDGE_ROWS, LANES))],
        out_shape=[
            jax.ShapeDtypeStruct((total, channels), BF16),
            jax.ShapeDtypeStruct((EDGE_ROWS, LANES), F32),
        ],
        scratch_shapes=[
            pltpu.VMEM((STATE, width), F32),
            pltpu.VMEM((-(-total // tok // EDGE_ROWS) * EDGE_ROWS, width), F32),
        ],
        input_output_aliases={0: 0} if alias else {},
        compiler_params=params(),
        cost_estimate=cost(6 * total * STATE * width, 8 * total * width + 6 * total * STATE),
        name="emit",
    )(*alias, xc, u, s_loc, c, m, ec, pj, skip, *ends, *decays)


def shards(
    x_in,
    bc_in,
    dt_raw,
    dt_bias,
    a_log,
    d_skip,
    conv_x_weight,
    conv_x_bias,
    conv_bc_weight,
    conv_bc_bias,
):
    n = lax.axis_size("inner")
    n_slab = lax.axis_size("slab")
    heads_dev = HEADS // n
    channels = heads_dev * HEADDIM
    per_group = HEADS // GROUPS
    index = lax.axis_index("inner")
    me = index.astype(jnp.int32).reshape(1)

    middle = n // 2
    shifts = sorted(range(1, n), key=lambda s: abs(s - middle))

    def rotate(arrays, chosen):
        for s in chosen:
            arrays[s - 1] = lax.ppermute(
                arrays[s - 1], "inner", [(i, (i + s) % n) for i in range(n)]
            )

    def forward(a, by):
        return lax.ppermute(a, "slab", [(i, i + by) for i in range(n_slab - by)])

    def mine(v):
        return lax.dynamic_slice_in_dim(v, index * heads_dev, heads_dev, 0)

    def exchange(a):
        return lax.all_to_all(a, "inner", split_axis=0, concat_axis=0, tiled=True)

    def send(k, parts):
        if not by_permutes(k):
            return [exchange(parts[0])]
        rotate(parts, shifts)
        return parts

    widths = chunk_widths(channels)
    packed = pack_bc(bc_in, dt_raw, n, heads_dev, per_group)
    message = exchange(packed)
    edges = pack_edge(x_in, bc_in, n, channels, heads_dev, per_group)
    edges = [
        lax.ppermute(
            e, ("slab", "inner"), [(s * n + n - 1, (s + 1) * n + j) for s in range(n_slab - 1)]
        )
        for j, e in enumerate(edges)
    ]
    packed_x = pack_x(me, x_in, n, channels, widths)
    received = [send(k, parts) for k, parts in enumerate(packed_x)]
    skip = jnp.repeat(mine(d_skip), HEADDIM)[None, :]
    x_weight = lax.dynamic_slice_in_dim(conv_x_weight, index * channels, channels, 1)
    x_bias = lax.dynamic_slice_in_dim(conv_x_bias, index * channels, channels, 0)[None, :]
    edge = sum(edges)
    bt, c, m, wu, ec, dj, pj, dv = prepare(
        me,
        message,
        edge[:, channels:],
        conv_bc_weight,
        conv_bc_bias[None, :],
        mine(dt_bias)[:, None],
        mine(a_log)[:, None],
        n,
        heads_dev,
        per_group,
    )
    decays = [forward(dv, by) for by in range(1, n_slab - 1)]
    y = None
    tokens, pending = [], []

    def finish():
        k, xc, u, s_loc, ends = pending.pop(0)
        return emit(
            y, xc, u, s_loc, c, m, ec, pj, ends, decays, skip, channels, widths[k], sum(widths[:k])
        )

    last = len(widths) - 1
    for k, width in enumerate(widths):
        first = sum(widths[:k])
        xc, u, s_loc, end = convolve(
            me,
            x_in,
            received[k],
            edge,
            x_weight,
            x_bias,
            bt,
            wu,
            dj,
            n,
            channels,
            width,
            first,
            decays if k == 0 else tokens[-1:],
        )
        ends = [forward(end, by) for by in range(1, n_slab)]
        pending.append((k, xc, u, s_loc, ends))
        while pending and (len(pending) > 1 or k in (0, last)):
            y, token = finish()
            tokens.append(token)
    return y


def solution(mesh):
    tokens = P(("slab", "inner"), None)
    placed = (tokens, tokens, tokens) + (P(),) * 7

    return jax.shard_map(
        shards, mesh=mesh, in_specs=placed, out_specs=P("slab", "inner"), check_vma=False
    )
```
